128 devices in a mesh: batch: 4 (over y), seq: 32 (over z, x, core).
Axes of the slice: x: 4, y: 4, z: 4, core: 2. Of those that a mesh axis runs over, the one named last changes fastest.
Arguments:
- queries: bfloat16 [4, 8192, 1024], P('batch', 'seq'), may hold values from -6 to 6
- key_states: bfloat16 [4, 8192, 1024], P('batch', 'seq'), may hold values from -6 to 6
- value_states: bfloat16 [4, 8192, 1024], P('batch', 'seq'), may hold values from -6 to 6
- out_grad: bfloat16 [4, 8192, 1024], P('batch', 'seq'), may hold values from -6 to 6
- memory: float32 [1024, 1024], replicated, may hold values from -6 to 6
- near_device: int32 [64, 8], replicated, may hold values from 0 to 31, all different within a row; in each aligned block of 2 rows (0 to 1, 2 to 3, ...) no two rows name the same one
- near_slot: int32 [64, 8], replicated, may hold values from 0 to 1
- near_count: int32 [64], replicated, may hold values from 1 to 8, 288 in all
- writer_block: int32 [1024], replicated, may hold values from 0 to 63, as said below
Outputs:
- attended: bfloat16 [4, 8192, 1024], P('batch', 'seq')
- query_grad: bfloat16 [4, 8192, 1024], P('batch', 'seq')
- key_grad: bfloat16 [4, 8192, 1024], P('batch', 'seq')
- value_grad: bfloat16 [4, 8192, 1024], P('batch', 'seq')
- memory_grad: float32 [1024, 1024], P('seq')
The draws below stay inside these ranges and needn't reach their ends.
Inputs may be any that keep to these rules, and one draw needn't show every extreme that they name: Row n of near_device belongs to block n; one row names different indices; the rows of the 2 blocks of one index of seq name no index more than 1 times. writer_block[r] // 2 == r // 32: a memory row is written by a block of the index of seq that holds the row.
All inputs are finite; a program needn't handle non-finite values.
Results may differ from the reference program's by a relative error of at most 0.025.
Values may be sent and summed in bfloat16 or wider, within the bound.
No kernel may reach another device: no remote copies, remote signals or barrier semaphores. Data moves between devices by JAX's collectives and lax.ppermute only.
A program may use at most 192 MiB of HBM per device.

```python
import math
import jax
import jax.numpy as jnp
import numpy as np
from jax import lax

HEADS = 8
HD = 128
BLK = 128
NEAR = 8
MEM = 1024
HW = 1024
BLK_DEV = 2
SEQ = 8192
BLOCKS = 64
BATCH = 4
ROWS_DEV = 32
CAP = 1
N_SEQ = 32


def draw_queries(key, part):
    base_key = jax.random.fold_in(key, 11)
    return jnp.clip(jax.random.normal(base_key, (BATCH, SEQ, HW), jnp.float32), -6.0, 6.0).astype(jnp.bfloat16)


def draw_memory(key, part):
    base_key = jax.random.fold_in(key, 23)
    return jnp.clip(jax.random.normal(base_key, (MEM, HW), jnp.float32), -6.0, 6.0)


def draw_writer_block(key, part):
    row_index = jnp.arange(MEM, dtype=jnp.int32)
    within = row_index % ROWS_DEV
    chosen_slot = jax.random.randint(jax.random.fold_in(key, 37), (MEM,), 0, BLK_DEV, dtype=jnp.int32)
    chosen_slot = jnp.where(within == 0, 0, jnp.where(within == ROWS_DEV - 1, BLK_DEV - 1, chosen_slot))
    return (row_index // ROWS_DEV * BLK_DEV + chosen_slot).astype(jnp.int32)


def plant(values, rng, low, largest):
    index_at = [jax.random.randint(jax.random.fold_in(rng, axis), (), 0, length) for axis, length in enumerate(values.shape)]
    main_axis = values.shape.index(max(values.shape))
    neighbour = index_at[:main_axis] + [(index_at[main_axis] + 1) % values.shape[main_axis]] + index_at[main_axis + 1:]
    return values.at[tuple(index_at)].set(low).at[tuple(neighbour)].set(largest)


def steps_of(key, dims, split, low, high):
    def one(axis_at, shards_of):
        steps = jax.random.uniform(jax.random.fold_in(jax.random.fold_in(key, 6), axis_at), (shards_of,), jnp.float32, low / len(split), high / len(split))
        return jnp.repeat(jnp.exp(steps), dims[axis_at] // shards_of).reshape((-1,) + (1,) * (len(dims) - axis_at - 1))

    gain = one(*split[0])
    for cut in split[1:]:
        gain = gain * one(*cut)
    return gain


def length_profile(count, total, most, slope):
    loads = [(1 << 20) // math.isqrt(standing ** slope) + 1 for standing in range(2, count + 1)]
    surplus, holding = total - most - (count - 1), [1] * (count - 1)
    while surplus > 0:
        candidates = [i for i in range(count - 1) if holding[i] < most]
        pool, budget = sum([loads[i] for i in candidates]), surplus
        for i in candidates:
            more = min(most - holding[i], max(1, budget * loads[i] // pool), surplus)
            holding[i] = holding[i] + more
            surplus = surplus - more
    return np.array([most] + holding)


def uneven_parts(rng, amount, total, bound, lean):
    if amount == 2:
        one = jax.random.randint(rng, (), max(1, total - bound), min(bound, total - 1) + 1)
        return jnp.stack([one, total - one])
    sizes = jnp.asarray(length_profile(amount, total, bound, lean), jnp.int32)
    couples = (amount - 1) // 2
    source_of, sink = sizes[1:1 + 2 * couples:2], sizes[2:2 + 2 * couples:2]
    room = jnp.minimum(source_of - 1, bound - sink)
    shifted = jax.random.randint(jax.random.fold_in(rng, 1), (couples,), 0, 1 << 20) % (room + 1)
    sizes = sizes.at[1:1 + 2 * couples:2].set(source_of - shifted).at[2:2 + 2 * couples:2].set(sink + shifted)
    return sizes[jax.random.permutation(jax.random.fold_in(rng, 2), amount)]


def shared_out(stream_key, own, number, rows, number_of, top, bound, slope):
    ranking = jax.random.permutation(stream_key, number_of)
    packed, ordinary = load_shares(number_of, rows * top, bound, slope, True), load_shares(number_of, rows * top, bound, slope, False)
    places = jnp.arange(number_of)

    def named(sizes, offset_by):
        used = int((sizes > 0).sum())
        fixed = max(1, used // 4)
        moved = fixed + (places - fixed + offset_by * (used - fixed)) % max(1, number_of - fixed)
        return jnp.zeros((number_of,), jnp.int32).at[ranking[jnp.where(places < fixed, places, moved)]].set(jnp.asarray(sizes, jnp.int32))

    sizes = jnp.where(number % 4 == 0, named(packed, number // 4), named(ordinary, number - number // 4 - 1))
    mixed = jax.random.permutation(jax.random.fold_in(own, 3), number_of)
    giver, taker = mixed[0:number_of // 2 * 2:2], mixed[1:number_of // 2 * 2:2]
    margin = jnp.minimum(sizes[giver] - 1, bound - sizes[taker]) // 2
    margin = jnp.where((giver == ranking[0]) | (taker == ranking[0]) | (sizes[taker] == 0), 0, jnp.maximum(margin, 0))
    moved = jax.random.randint(jax.random.fold_in(own, 4), (number_of // 2,), 0, 1 << 20) % (margin + 1)
    sizes = sizes.at[giver].add(-moved).at[taker].add(moved)
    items = jnp.searchsorted(jnp.cumsum(sizes), jnp.arange(rows * top), side="right").astype(jnp.int32)
    table = items.reshape(top, rows).T
    table = table[jax.random.permutation(jax.random.fold_in(own, 1), rows)]
    offset_by = jax.random.randint(jax.random.fold_in(own, 2), (rows, 1), 0, top)
    return jnp.take_along_axis(table, (jnp.arange(top)[None, :] + offset_by) % top, axis=1)


def load_shares(number_of, total, reach, lean, full):
    weights = [(1 << 20) // math.isqrt(grade ** lean) + 1 for grade in range(1, number_of + 1)]
    largest = reach if full else min(reach, max(-(-total // number_of), total * weights[0] // sum(weights)))
    least = 1 if total - largest >= number_of - 1 else 0
    holding, surplus = [largest] + [least] * (number_of - 1), total - largest - least * (number_of - 1)
    while surplus > 0:
        movable = [i for i in range(1, number_of) if holding[i] < largest] or [i for i in range(1, number_of) if holding[i] < reach]
        whole, left = sum([weights[i] for i in movable]), surplus
        for i in movable:
            extra = min(reach - holding[i], max(1, left * weights[i] // whole), surplus)
            holding[i] = holding[i] + extra
            surplus = surplus - extra
    return np.array(holding)


def gaussian(key, shape, width, reach, shards=(), held_as=jnp.bfloat16):
    values = jax.random.normal(key, shape, jnp.float32) * width
    if len(shards) > 0:
        values = steps_of(key, shape, shards, -0.22, 0.18) * values
    return jnp.clip(values, min=-reach, max=reach).astype(held_as)


def setup_inputs(seed: int = 0) -> dict:
    arg_keys = jax.random.split(jax.random.key(seed), 10)
    queries = draw_queries(jax.random.fold_in(arg_keys[9], 71), 0)
    key_states = gaussian(arg_keys[1], (BATCH, SEQ, HW), 1.0, 6.0, ((0, 4), (1, 32)))
    value_states = gaussian(arg_keys[2], (BATCH, SEQ, HW), 1.0, 6.0, ((0, 4), (1, 32)))
    out_grad = gaussian(arg_keys[3], (BATCH, SEQ, HW), 1.0, 6.0, ((0, 4), (1, 32)))
    memory = draw_memory(jax.random.fold_in(arg_keys[9], 71), 0)
    near_device_keys = jax.random.split(jax.random.fold_in(arg_keys[5], 1), BLOCKS // BLK_DEV)
    near_device_turns = jax.random.permutation(jax.random.fold_in(arg_keys[5], 3), BLOCKS // BLK_DEV)
    near_device = jax.vmap(lambda own, number: shared_out(jax.random.fold_in(arg_keys[5], 2), own, number, BLK_DEV, N_SEQ, NEAR, CAP, 2))(near_device_keys, near_device_turns).reshape((BLOCKS, NEAR))
    near_slot = plant(jax.random.randint(arg_keys[6], (BLOCKS, NEAR), 0, BLK_DEV), jax.random.fold_in(arg_keys[6], 1), 0, BLK_DEV - 1).astype(jnp.int32)
    near_count = uneven_parts(arg_keys[7], BLOCKS, BLOCKS * (NEAR + 1) // 2, NEAR, 2).astype(jnp.int32)
    writer_block = draw_writer_block(jax.random.fold_in(arg_keys[9], 71), 0)
    return dict(queries=queries, key_states=key_states, value_states=value_states, out_grad=out_grad, memory=memory, near_device=near_device, near_slot=near_slot, near_count=near_count, writer_block=writer_block)


def rounded_width(value):
    return lax.optimization_barrier(value.astype(jnp.bfloat16))

def reference(queries, key_states, value_states, out_grad, memory, near_device, near_slot, near_count, writer_block):
    key_scaling_factor = 1.0 / math.sqrt(HD)
    block_scale = 1.0 / math.sqrt(BLK)
    near_block = (near_device * BLK_DEV + near_slot).astype(jnp.int32)

    def one_batch(inputs):
        query_rows, key_rows, value_rows, grad_rows = inputs
        value_sums = lax.optimization_barrier(jnp.sum(value_rows.reshape(BLOCKS, BLK, HW).astype(jnp.float32), axis=1))
        memory_keys = rounded_width(memory + value_sums[writer_block] * block_scale)
        memory_head_states = memory_keys.astype(jnp.float32).reshape(MEM, HEADS, HD)
        key_blocks = key_rows.reshape(BLOCKS, BLK, HW)
        value_blocks = value_rows.reshape(BLOCKS, BLK, HW)

        def one_block(grad_total, block_index):
            start = (block_index * BLK).astype(jnp.int32)
            query_head_states = lax.dynamic_slice_in_dim(query_rows, start, BLK, 0).astype(jnp.float32).reshape(BLK, HEADS, HD)
            head_output_gradient = lax.dynamic_slice_in_dim(grad_rows, start, BLK, 0).astype(jnp.float32).reshape(BLK, HEADS, HD)
            chosen = near_block[block_index]
            neighbour_key_rows = jnp.take(key_blocks, chosen, axis=0).astype(jnp.float32).reshape(NEAR * BLK, HEADS, HD)
            neighbour_value_rows = jnp.take(value_blocks, chosen, axis=0).astype(jnp.float32).reshape(NEAR * BLK, HEADS, HD)
            live_keys = jnp.arange(NEAR * BLK, dtype=jnp.int32) // BLK < near_count[block_index]
            memory_score_logits = jnp.einsum('lan,san->als', query_head_states, memory_head_states) * key_scaling_factor
            score_near = jnp.einsum('qhd,khd->hqk', query_head_states, neighbour_key_rows) * key_scaling_factor
            score_near = jnp.where(live_keys[None, None, :], score_near, -jnp.inf)
            row_max = jnp.maximum(lax.optimization_barrier(jnp.max(memory_score_logits, axis=-1)), lax.optimization_barrier(jnp.max(score_near, axis=-1)))
            exp_mem = jnp.exp(memory_score_logits - row_max[:, :, None])
            exp_near = jnp.exp(score_near - row_max[:, :, None])
            row_total = lax.optimization_barrier(jnp.sum(exp_mem, axis=-1)) + lax.optimization_barrier(jnp.sum(exp_near, axis=-1))
            prob_mem = exp_mem / row_total[:, :, None]
            prob_near = exp_near / row_total[:, :, None]
            memory_attention_weight = rounded_width(prob_mem).astype(jnp.float32)
            neighbour_attention_weight = rounded_width(prob_near).astype(jnp.float32)
            head_attended_output = rounded_width(jnp.einsum('ywo,oya->wya', memory_attention_weight, memory_head_states) + jnp.einsum('wpg,gwm->pwm', neighbour_attention_weight, neighbour_value_rows))
            grad_dot = lax.optimization_barrier(jnp.sum(head_output_gradient * head_attended_output.astype(jnp.float32), axis=-1)).T
            memory_probability_gradient = jnp.einsum('lan,san->als', head_output_gradient, memory_head_states)
            dprob_near = jnp.einsum('qhd,khd->hqk', head_output_gradient, neighbour_value_rows)
            memory_score_gradient = rounded_width(prob_mem * (memory_probability_gradient - grad_dot[:, :, None])).astype(jnp.float32)
            neighbour_score_gradient = rounded_width(prob_near * (dprob_near - grad_dot[:, :, None])).astype(jnp.float32)
            query_portion = rounded_width((jnp.einsum('ywo,oya->wya', memory_score_gradient, memory_head_states) + jnp.einsum('wpg,gwm->pwm', neighbour_score_gradient, neighbour_key_rows)) * key_scaling_factor)
            memory_contribution = jnp.einsum('toi,otl->itl', memory_score_gradient, query_head_states) * key_scaling_factor + jnp.einsum('toi,otl->itl', memory_attention_weight, head_output_gradient)
            key_parts = rounded_width(jnp.einsum('hqk,qhd->khd', neighbour_score_gradient, query_head_states) * key_scaling_factor).reshape(NEAR, BLK, HW)
            value_parts = rounded_width(jnp.einsum('hqk,qhd->khd', neighbour_attention_weight, head_output_gradient)).reshape(NEAR, BLK, HW)
            outputs = (head_attended_output.reshape(BLK, HW), query_portion.reshape(BLK, HW), key_parts, value_parts)
            return (grad_total + memory_contribution.reshape(MEM, HW), outputs)
        start_total = jnp.zeros((MEM, HW), jnp.float32)
        row_grad, stacked = lax.scan(one_block, start_total, jnp.arange(BLOCKS, dtype=jnp.int32))
        attended_rows, query_rows_grad, key_parts, value_parts = stacked
        flat_blocks = near_block.reshape(BLOCKS * NEAR)
        key_sum = jnp.zeros((BLOCKS, BLK, HW), jnp.float32).at[flat_blocks].add(key_parts.reshape(BLOCKS * NEAR, BLK, HW).astype(jnp.float32))
        value_sum = jnp.zeros((BLOCKS, BLK, HW), jnp.float32).at[flat_blocks].add(value_parts.reshape(BLOCKS * NEAR, BLK, HW).astype(jnp.float32))
        spread = jax.ops.segment_sum(row_grad, writer_block, num_segments=BLOCKS) * block_scale
        key_out = key_sum.astype(jnp.bfloat16).reshape(SEQ, HW)
        value_out = (value_sum + spread[:, None, :]).astype(jnp.bfloat16).reshape(SEQ, HW)
        return (attended_rows.reshape(SEQ, HW), query_rows_grad.reshape(SEQ, HW), key_out, value_out, row_grad)
    attended, query_grad, key_grad, value_grad, row_grads = lax.map(one_batch, (queries, key_states, value_states, out_grad))
    return (attended, query_grad, key_grad, value_grad, lax.optimization_barrier(jnp.sum(row_grads, axis=0)))
```

```python
import math

import jax
import jax.numpy as jnp
from jax import lax
from jax.sharding import PartitionSpec as P

HEADS = 8
HD = 128
BLK = 128
MEM = 1024


def shards(
    queries,
    key_states,
    value_states,
    out_grad,
    memory,
    near_device,
    near_slot,
    near_count,
    writer_block,
):
    seq_devices = lax.axis_size("seq")
    batch_devices = lax.axis_size("batch")
    my_index = lax.axis_index("seq")
    tokens = queries.shape[1]
    row_width = queries.shape[2]
    near_width = near_device.shape[1]
    local_blocks = tokens // BLK
    entries = local_blocks * near_width
    rows_dev = MEM // seq_devices
    key_scaling_factor = 1.0 / math.sqrt(HD)
    block_scale = 1.0 / math.sqrt(BLK)
    value_blocks = value_states[0].reshape(local_blocks, BLK, row_width)
    key_blocks = key_states[0].reshape(local_blocks, BLK, row_width)

    target = near_device.reshape(seq_devices, entries)
    source_slot = near_slot.reshape(seq_devices, entries)
    my_target = lax.dynamic_index_in_dim(target, my_index, 0, keepdims=False)
    names_me = target == my_index
    send_idx = jnp.sum(jnp.where(names_me, source_slot, 0), axis=1)
    kv_blocks = jnp.stack([key_blocks, value_blocks], axis=1)
    send_kv = jnp.take(kv_blocks, send_idx, axis=0)
    got_kv = lax.all_to_all(send_kv, "seq", split_axis=0, concat_axis=0, tiled=True)

    value_sums = jnp.sum(value_blocks, axis=1, dtype=jnp.float32)
    all_sums = lax.all_to_all(
        jnp.broadcast_to(value_sums[None], (seq_devices, local_blocks, row_width)),
        "seq",
        split_axis=0,
        concat_axis=0,
        tiled=True,
    ).reshape(seq_devices * local_blocks, row_width)
    memory_keys = (memory + jnp.take(all_sums, writer_block, axis=0) * block_scale).astype(
        jnp.bfloat16
    )

    neighbour_kv = jnp.take(got_kv, my_target, axis=0)
    neighbour_key_rows = neighbour_kv[:, 0].reshape(local_blocks, near_width * BLK, HEADS, HD)
    neighbour_value_rows = neighbour_kv[:, 1].reshape(local_blocks, near_width * BLK, HEADS, HD)
    my_count = lax.dynamic_slice_in_dim(near_count, my_index * local_blocks, local_blocks, 0)
    live_keys = jnp.arange(near_width * BLK)[None, :] // BLK < my_count[:, None]
    query_head_states = queries[0].reshape(local_blocks, BLK, HEADS, HD)
    head_output_gradient = out_grad[0].reshape(local_blocks, BLK, HEADS, HD)
    memory_head_states = memory_keys.reshape(MEM, HEADS, HD)
    memory_score_logits = (
        jnp.einsum(
            "xswr,gwr->xwsg",
            query_head_states,
            memory_head_states,
            preferred_element_type=jnp.float32,
        )
        * key_scaling_factor
    )
    score_near = (
        jnp.einsum(
            "cqhd,ckhd->chqk",
            query_head_states,
            neighbour_key_rows,
            preferred_element_type=jnp.float32,
        )
        * key_scaling_factor
    )
    score_near = jnp.where(live_keys[:, None, None, :], score_near, -jnp.inf)
    row_max = jnp.maximum(jnp.max(memory_score_logits, axis=-1), jnp.max(score_near, axis=-1))
    exp_mem = jnp.exp(memory_score_logits - row_max[..., None])
    exp_near = jnp.exp(score_near - row_max[..., None])
    row_total = jnp.sum(exp_mem, axis=-1) + jnp.sum(exp_near, axis=-1)
    prob_mem = exp_mem / row_total[..., None]
    prob_near = exp_near / row_total[..., None]
    memory_attention_weight = prob_mem.astype(jnp.bfloat16)
    neighbour_attention_weight = prob_near.astype(jnp.bfloat16)
    head_attended_output = (
        jnp.einsum(
            "vjpe,eji->vpji",
            memory_attention_weight,
            memory_head_states,
            preferred_element_type=jnp.float32,
        )
        + jnp.einsum(
            "chqk,ckhd->cqhd",
            neighbour_attention_weight,
            neighbour_value_rows,
            preferred_element_type=jnp.float32,
        )
    ).astype(jnp.bfloat16)
    grad_dot = jnp.einsum(
        "cqhd,cqhd->chq",
        head_output_gradient,
        head_attended_output,
        preferred_element_type=jnp.float32,
    )
    memory_probability_gradient = jnp.einsum(
        "xswr,gwr->xwsg",
        head_output_gradient,
        memory_head_states,
        preferred_element_type=jnp.float32,
    )
    dprob_near = jnp.einsum(
        "cqhd,ckhd->chqk",
        head_output_gradient,
        neighbour_value_rows,
        preferred_element_type=jnp.float32,
    )
    memory_score_gradient = (prob_mem * (memory_probability_gradient - grad_dot[..., None])).astype(
        jnp.bfloat16
    )
    neighbour_score_gradient = (prob_near * (dprob_near - grad_dot[..., None])).astype(jnp.bfloat16)
    query_portion = (
        jnp.einsum(
            "vjpe,eji->vpji",
            memory_score_gradient,
            memory_head_states,
            preferred_element_type=jnp.float32,
        )
        + jnp.einsum(
            "chqk,ckhd->cqhd",
            neighbour_score_gradient,
            neighbour_key_rows,
            preferred_element_type=jnp.float32,
        )
    ) * key_scaling_factor
    key_part = (
        jnp.einsum(
            "chqk,cqhd->ckhd",
            neighbour_score_gradient,
            query_head_states,
            preferred_element_type=jnp.float32,
        )
        * key_scaling_factor
    ).astype(jnp.bfloat16)
    value_part = jnp.einsum(
        "chqk,cqhd->ckhd",
        neighbour_attention_weight,
        head_output_gradient,
        preferred_element_type=jnp.float32,
    ).astype(jnp.bfloat16)
    key_part = key_part.reshape(entries, BLK, row_width)
    value_part = value_part.reshape(entries, BLK, row_width)
    term = (
        jnp.einsum(
            "irey,ierk->yrk",
            memory_score_gradient,
            query_head_states,
            preferred_element_type=jnp.float32,
        )
        * key_scaling_factor
    )
    term = term + jnp.einsum(
        "irey,ierk->yrk",
        memory_attention_weight,
        head_output_gradient,
        preferred_element_type=jnp.float32,
    )
    term = term.reshape(seq_devices, rows_dev, row_width).astype(jnp.bfloat16)

    hits = my_target[None, :] == jnp.arange(seq_devices)[:, None]
    inverse = jnp.sum(jnp.where(hits, jnp.arange(entries)[None, :], 0), axis=1)
    valid = jnp.any(hits, axis=1)[:, None, None]
    back_keys = jnp.where(valid, jnp.take(key_part, inverse, axis=0), jnp.zeros((), jnp.bfloat16))
    back_values = jnp.where(valid, jnp.take(value_part, inverse, axis=0), jnp.zeros((), jnp.bfloat16))
    back = jnp.concatenate([back_keys, back_values, term], axis=1)
    got_back = lax.all_to_all(back, "seq", split_axis=0, concat_axis=0, tiled=True)
    select = jnp.sum(
        jnp.where(
            names_me[:, :, None],
            (source_slot[:, :, None] == jnp.arange(local_blocks)[None, None, :]).astype(jnp.float32),
            0.0,
        ),
        axis=1,
    ).astype(jnp.bfloat16)
    key_sum = jnp.einsum(
        "dl,dtw->ltw", select, got_back[:, :BLK], preferred_element_type=jnp.float32
    )
    value_sum = jnp.einsum(
        "dl,dtw->ltw", select, got_back[:, BLK : 2 * BLK], preferred_element_type=jnp.float32
    )
    row_grads = jnp.sum(got_back[:, 2 * BLK :].astype(jnp.float32), axis=0)
    my_writers = (
        lax.dynamic_slice_in_dim(writer_block, my_index * rows_dev, rows_dev, 0)
        - my_index * local_blocks
    )
    writer_match = (my_writers[:, None] == jnp.arange(local_blocks)[None, :])[:, :, None]
    spread = jnp.sum(jnp.where(writer_match, row_grads[:, None, :], 0.0), axis=0) * block_scale
    all_rows = lax.all_to_all(
        jnp.broadcast_to(row_grads[None], (batch_devices, rows_dev, row_width)),
        "batch",
        split_axis=0,
        concat_axis=0,
        tiled=True,
    )
    memory_grad = jnp.sum(all_rows, axis=0)
    attended = head_attended_output.reshape(1, tokens, row_width)
    query_grad = query_portion.astype(jnp.bfloat16).reshape(1, tokens, row_width)
    key_grad = key_sum.astype(jnp.bfloat16).reshape(1, tokens, row_width)
    value_grad = (value_sum + spread[:, None, :]).astype(jnp.bfloat16).reshape(1, tokens, row_width)
    return (attended, query_grad, key_grad, value_grad, memory_grad)


def solution(mesh):
    placed = (
        P("batch", "seq", None),
        P("batch", "seq", None),
        P("batch", "seq", None),
        P("batch", "seq", None),
        P(),
        P(),
        P(),
        P(),
        P(),
    )
    return jax.shard_map(
        shards,
        mesh=mesh,
        in_specs=placed,
        out_specs=(
            P("batch", "seq", None),
            P("batch", "seq", None),
            P("batch", "seq", None),
            P("batch", "seq", None),
            P("seq", None),
        ),
        check_vma=False,
    )
```

```python
import math

import jax
import jax.numpy as jnp
from jax import lax
from jax.experimental import pallas as pl
from jax.experimental.pallas import tpu as pltpu
from jax.sharding import PartitionSpec as P

HEADS = 8
HD = 128
BLK = 128
MEM = 1024
NEAR = 8


def _attn_body(cnt_ref, tgt_ref, q_ref, do_ref, mk_ref, *rest):
    k_refs = rest[:NEAR]
    v_refs = rest[NEAR : 2 * NEAR]
    o_ref, dq_ref, dk_ref, dv_ref, tm_ref = rest[2 * NEAR :]
    n = pl.program_id(1)
    scale = 1.0 / math.sqrt(HD)
    f32 = jnp.float32
    nt = (((1,), (1,)), ((), ()))
    tn = (((0,), (0,)), ((), ()))
    q = q_ref[...]
    do = do_ref[...]
    mk = mk_ref[...]
    nk = jnp.concatenate([r[0, 0] for r in k_refs], axis=0)
    nv = jnp.concatenate([r[0, 0] for r in v_refs], axis=0)
    sm = lax.dot_general(q, mk, nt, preferred_element_type=f32) * scale
    sn = lax.dot_general(q, nk, nt, preferred_element_type=f32) * scale
    col = lax.broadcasted_iota(jnp.int32, sn.shape, 1) // BLK
    sn = jnp.where(col < cnt_ref[n], sn, -jnp.inf)
    m = jnp.maximum(jnp.max(sm, axis=1, keepdims=True), jnp.max(sn, axis=1, keepdims=True))
    em = jnp.exp(sm - m)
    en = jnp.exp(sn - m)
    total = jnp.sum(em, axis=1, keepdims=True) + jnp.sum(en, axis=1, keepdims=True)
    pm = em / total
    pn = en / total
    wm = pm.astype(jnp.bfloat16)
    wn = pn.astype(jnp.bfloat16)
    o = (
        jnp.dot(wm, mk, preferred_element_type=f32) + jnp.dot(wn, nv, preferred_element_type=f32)
    ).astype(jnp.bfloat16)
    o_ref[...] = o
    gd = jnp.sum(do.astype(f32) * o.astype(f32), axis=1, keepdims=True)
    dpm = lax.dot_general(do, mk, nt, preferred_element_type=f32)
    dpn = lax.dot_general(do, nv, nt, preferred_element_type=f32)
    dsm = (pm * (dpm - gd)).astype(jnp.bfloat16)
    dsn = (pn * (dpn - gd)).astype(jnp.bfloat16)
    dq_ref[...] = (
        (jnp.dot(dsm, mk, preferred_element_type=f32) + jnp.dot(dsn, nk, preferred_element_type=f32))
        * scale
    ).astype(jnp.bfloat16)
    dk_ref[0] = (lax.dot_general(dsn, q, tn, preferred_element_type=f32) * scale).astype(jnp.bfloat16)
    dv_ref[0] = lax.dot_general(wn, do, tn, preferred_element_type=f32).astype(jnp.bfloat16)
    tm = lax.dot_general(dsm, q, tn, preferred_element_type=f32) * scale + lax.dot_general(
        wm, do, tn, preferred_element_type=f32
    )

    @pl.when(n == 0)
    def _():
        tm_ref[...] = tm

    @pl.when(n != 0)
    def _():
        tm_ref[...] += tm


def attention_core(counts, targets, q, do, mk, got_kv):
    tokens, width = q.shape
    blocks = tokens // BLK
    mem = mk.shape[0]
    heads = width // HD
    nrows = NEAR * BLK
    qspec = pl.BlockSpec((BLK, HD), lambda h, n, c, t: (n, h))
    mspec = pl.BlockSpec((mem, HD), lambda h, n, c, t: (0, h))

    def kv_spec(j, which):
        return pl.BlockSpec((1, 1, BLK, HD), lambda h, n, c, t: (t[n * NEAR + j], which, 0, h))

    nspec = pl.BlockSpec((1, nrows, HD), lambda h, n, c, t: (n, 0, h))
    flops = 2 * tokens * width * (mem + nrows) * 4 + 2 * tokens * width * (nrows * 2 + mem * 2)
    grid_spec = pltpu.PrefetchScalarGridSpec(
        num_scalar_prefetch=2,
        grid=(heads, blocks),
        in_specs=[qspec, qspec, mspec]
        + [kv_spec(j, 0) for j in range(NEAR)]
        + [kv_spec(j, 1) for j in range(NEAR)],
        out_specs=[qspec, qspec, nspec, nspec, mspec],
    )
    return pl.pallas_call(
        _attn_body,
        grid_spec=grid_spec,
        out_shape=[
            jax.ShapeDtypeStruct((tokens, width), jnp.bfloat16),
            jax.ShapeDtypeStruct((tokens, width), jnp.bfloat16),
            jax.ShapeDtypeStruct((blocks, nrows, width), jnp.bfloat16),
            jax.ShapeDtypeStruct((blocks, nrows, width), jnp.bfloat16),
            jax.ShapeDtypeStruct((mem, width), jnp.float32),
        ],
        compiler_params=pltpu.CompilerParams(dimension_semantics=("arbitrary", "arbitrary")),
        cost_estimate=pl.CostEstimate(
            flops=flops,
            transcendentals=tokens * heads * (mem + nrows),
            bytes_accessed=2 * (4 * tokens * width + mem * width + 4 * blocks * nrows * width)
            + 4 * mem * width,
        ),
    )(counts, targets, q, do, mk, *([got_kv] * (2 * NEAR)))


def shards(
    queries,
    key_states,
    value_states,
    out_grad,
    memory,
    near_device,
    near_slot,
    near_count,
    writer_block,
):
    seq_devices = lax.axis_size("seq")
    batch_devices = lax.axis_size("batch")
    my_index = lax.axis_index("seq")
    tokens = queries.shape[1]
    row_width = queries.shape[2]
    near_width = near_device.shape[1]
    local_blocks = tokens // BLK
    entries = local_blocks * near_width
    rows_dev = MEM // seq_devices
    key_scaling_factor = 1.0 / math.sqrt(HD)
    block_scale = 1.0 / math.sqrt(BLK)
    value_blocks = value_states[0].reshape(local_blocks, BLK, row_width)
    key_blocks = key_states[0].reshape(local_blocks, BLK, row_width)

    target = near_device.reshape(seq_devices, entries)
    source_slot = near_slot.reshape(seq_devices, entries)
    my_target = lax.dynamic_index_in_dim(target, my_index, 0, keepdims=False)
    names_me = target == my_index
    send_idx = jnp.sum(jnp.where(names_me, source_slot, 0), axis=1)
    kv_blocks = jnp.stack([key_blocks, value_blocks], axis=1)
    send_kv = jnp.take(kv_blocks, send_idx, axis=0)
    got_kv = lax.all_to_all(send_kv, "seq", split_axis=0, concat_axis=0, tiled=True)

    value_sums = jnp.sum(value_blocks, axis=1, dtype=jnp.float32)
    all_sums = lax.all_to_all(
        jnp.broadcast_to(value_sums[None], (seq_devices, local_blocks, row_width)),
        "seq",
        split_axis=0,
        concat_axis=0,
        tiled=True,
    ).reshape(seq_devices * local_blocks, row_width)
    memory_keys = (memory + jnp.take(all_sums, writer_block, axis=0) * block_scale).astype(
        jnp.bfloat16
    )

    my_count = lax.dynamic_slice_in_dim(near_count, my_index * local_blocks, local_blocks, 0)
    attended_rows, query_rows_grad, key_part, value_part, term = attention_core(
        my_count, my_target, queries[0], out_grad[0], memory_keys, got_kv
    )
    key_part = key_part.reshape(entries, BLK, row_width)
    value_part = value_part.reshape(entries, BLK, row_width)
    term = term.reshape(seq_devices, rows_dev, row_width).astype(jnp.bfloat16)

    hits = my_target[None, :] == jnp.arange(seq_devices)[:, None]
    inverse = jnp.sum(jnp.where(hits, jnp.arange(entries)[None, :], 0), axis=1)
    back_keys = jnp.take(key_part, inverse, axis=0)
    back_values = jnp.take(value_part, inverse, axis=0)
    back = jnp.concatenate([back_keys, back_values, term], axis=1)
    got_back = lax.all_to_all(back, "seq", split_axis=0, concat_axis=0, tiled=True)
    select = jnp.sum(
        jnp.where(
            names_me[:, :, None],
            (source_slot[:, :, None] == jnp.arange(local_blocks)[None, None, :]).astype(jnp.float32),
            0.0,
        ),
        axis=1,
    ).astype(jnp.bfloat16)
    key_sum = jnp.einsum(
        "dl,dtw->ltw", select, got_back[:, :BLK], preferred_element_type=jnp.float32
    )
    value_sum = jnp.einsum(
        "dl,dtw->ltw", select, got_back[:, BLK : 2 * BLK], preferred_element_type=jnp.float32
    )
    row_grads = jnp.sum(got_back[:, 2 * BLK :].astype(jnp.float32), axis=0)
    my_writers = (
        lax.dynamic_slice_in_dim(writer_block, my_index * rows_dev, rows_dev, 0)
        - my_index * local_blocks
    )
    writer_match = (my_writers[:, None] == jnp.arange(local_blocks)[None, :])[:, :, None]
    spread = jnp.sum(jnp.where(writer_match, row_grads[:, None, :], 0.0), axis=0) * block_scale
    all_rows = lax.all_to_all(
        jnp.broadcast_to(row_grads[None], (batch_devices, rows_dev, row_width)),
        "batch",
        split_axis=0,
        concat_axis=0,
        tiled=True,
    )
    memory_grad = jnp.sum(all_rows, axis=0)
    attended = attended_rows.reshape(1, tokens, row_width)
    query_grad = query_rows_grad.reshape(1, tokens, row_width)
    key_grad = key_sum.astype(jnp.bfloat16).reshape(1, tokens, row_width)
    value_grad = (value_sum + spread[:, None, :]).astype(jnp.bfloat16).reshape(1, tokens, row_width)
    return (attended, query_grad, key_grad, value_grad, memory_grad)


def solution(mesh):
    placed = (
        P("batch", "seq", None),
        P("batch", "seq", None),
        P("batch", "seq", None),
        P("batch", "seq", None),
        P(),
        P(),
        P(),
        P(),
        P(),
    )
    return jax.shard_map(
        shards,
        mesh=mesh,
        in_specs=placed,
        out_specs=(
            P("batch", "seq", None),
            P("batch", "seq", None),
            P("batch", "seq", None),
            P("batch", "seq", None),
            P("seq", None),
        ),
        check_vma=False,
    )
```

```python
import math

import jax
import jax.numpy as jnp
from jax import lax
from jax.experimental import pallas as pl
from jax.experimental.pallas import tpu as pltpu
from jax.sharding import PartitionSpec as P

HEADS = 8
HD = 128
BLK = 128
MEM = 1024
NEAR = 8


def _attn_body(cnt_ref, nb_ref, q_ref, do_ref, mk_ref, *rest):
    k_refs = rest[:NEAR]
    v_refs = rest[NEAR : 2 * NEAR]
    _, o_ref, dq_ref, tm_ref, dkv_hbm, dks, dvs, sems = rest[2 * NEAR :]
    h = pl.program_id(0)
    n = pl.program_id(1)
    blocks = pl.num_programs(1)
    steps = pl.num_programs(0) * blocks
    step = h * blocks + n
    slot = step % 2
    heads = pl.num_programs(0)
    scale = 1.0 / math.sqrt(HD)
    f32 = jnp.float32
    nt = (((1,), (1,)), ((), ()))
    tn = (((0,), (0,)), ((), ()))
    q = q_ref[...]
    do = do_ref[...]
    mk = mk_ref[...]
    nk = jnp.concatenate([r[...] for r in k_refs], axis=0)
    nv = jnp.concatenate([r[...] for r in v_refs], axis=0)
    sm = lax.dot_general(q, mk, nt, preferred_element_type=f32) * scale
    sn = lax.dot_general(q, nk, nt, preferred_element_type=f32) * scale
    col = lax.broadcasted_iota(jnp.int32, sn.shape, 1) // BLK
    sn = jnp.where(col < cnt_ref[n], sn, -jnp.inf)
    m = jnp.maximum(jnp.max(sm, axis=1, keepdims=True), jnp.max(sn, axis=1, keepdims=True))
    em = jnp.exp(sm - m)
    en = jnp.exp(sn - m)
    total = jnp.sum(em, axis=1, keepdims=True) + jnp.sum(en, axis=1, keepdims=True)
    pm = em / total
    pn = en / total
    wm = pm.astype(jnp.bfloat16)
    wn = pn.astype(jnp.bfloat16)
    o = (
        jnp.dot(wm, mk, preferred_element_type=f32) + jnp.dot(wn, nv, preferred_element_type=f32)
    ).astype(jnp.bfloat16)
    o_ref[...] = o
    gd = jnp.sum(do.astype(f32) * o.astype(f32), axis=1, keepdims=True)
    dpm = lax.dot_general(do, mk, nt, preferred_element_type=f32)
    dpn = lax.dot_general(do, nv, nt, preferred_element_type=f32)
    dsm = (pm * (dpm - gd)).astype(jnp.bfloat16)
    dsn = (pn * (dpn - gd)).astype(jnp.bfloat16)
    dq_ref[...] = (
        (jnp.dot(dsm, mk, preferred_element_type=f32) + jnp.dot(dsn, nk, preferred_element_type=f32))
        * scale
    ).astype(jnp.bfloat16)
    dk = (lax.dot_general(dsn, q, tn, preferred_element_type=f32) * scale).astype(jnp.bfloat16)
    dv = lax.dot_general(wn, do, tn, preferred_element_type=f32).astype(jnp.bfloat16)
    tm = lax.dot_general(dsm, q, tn, preferred_element_type=f32) * scale + lax.dot_general(
        wm, do, tn, preferred_element_type=f32
    )

    @pl.when(n == 0)
    def _():
        tm_ref[...] = tm

    @pl.when(n != 0)
    def _():
        tm_ref[...] += tm

    def copies(at_step, at_slot):
        at_h = at_step // blocks
        at_n = at_step % blocks
        out = []
        for j in range(NEAR):
            rows = pl.ds(pl.multiple_of(nb_ref[at_n * NEAR + j] * BLK, BLK), BLK)
            out.append(
                pltpu.make_async_copy(
                    dks.at[at_slot, j],
                    dkv_hbm.at[rows, pl.ds(pl.multiple_of(at_h * HD, HD), HD)],
                    sems.at[at_slot, j],
                )
            )
            out.append(
                pltpu.make_async_copy(
                    dvs.at[at_slot, j],
                    dkv_hbm.at[rows, pl.ds(pl.multiple_of((heads + at_h) * HD, HD), HD)],
                    sems.at[at_slot, NEAR + j],
                )
            )
        return out

    @pl.when(step >= 2)
    def _():
        for c in copies(step - 2, slot):
            c.wait()

    for j in range(NEAR):
        dks[slot, j] = dk[j * BLK : (j + 1) * BLK]
        dvs[slot, j] = dv[j * BLK : (j + 1) * BLK]
    for c in copies(step, slot):
        c.start()

    @pl.when(step == steps - 1)
    def _():
        for c in copies(step - 1, 1 - slot):
            c.wait()
        for c in copies(step, slot):
            c.wait()


def attention_core(counts, near_rows, q, do, mk, kv_all):
    tokens, width = q.shape
    blocks = tokens // BLK
    mem = mk.shape[0]
    heads = width // HD
    nrows = NEAR * BLK
    qspec = pl.BlockSpec((BLK, HD), lambda h, n, c, t: (n, h))
    mspec = pl.BlockSpec((mem, HD), lambda h, n, c, t: (0, h))

    def kv_spec(j, which):
        return pl.BlockSpec((BLK, HD), lambda h, n, c, t: (t[n * NEAR + j], which * heads + h))

    anyspec = pl.BlockSpec(memory_space=pl.ANY)
    flops = 2 * tokens * width * (mem + nrows) * 4 + 2 * tokens * width * (nrows * 2 + mem * 2)
    grid_spec = pltpu.PrefetchScalarGridSpec(
        num_scalar_prefetch=2,
        grid=(heads, blocks),
        in_specs=[qspec, qspec, mspec]
        + [kv_spec(j, 0) for j in range(NEAR)]
        + [kv_spec(j, 1) for j in range(NEAR)]
        + [anyspec],
        out_specs=[qspec, qspec, mspec, anyspec],
        scratch_shapes=[
            pltpu.VMEM((2, NEAR, BLK, HD), jnp.bfloat16),
            pltpu.VMEM((2, NEAR, BLK, HD), jnp.bfloat16),
            pltpu.SemaphoreType.DMA((2, 2 * NEAR)),
        ],
    )
    zeros = jnp.zeros(kv_all.shape, jnp.bfloat16)
    return pl.pallas_call(
        _attn_body,
        grid_spec=grid_spec,
        out_shape=[
            jax.ShapeDtypeStruct((tokens, width), jnp.bfloat16),
            jax.ShapeDtypeStruct((tokens, width), jnp.bfloat16),
            jax.ShapeDtypeStruct((mem, width), jnp.float32),
            jax.ShapeDtypeStruct(kv_all.shape, jnp.bfloat16),
        ],
        input_output_aliases={2 + 3 + 2 * NEAR: 3},
        compiler_params=pltpu.CompilerParams(dimension_semantics=("arbitrary", "arbitrary")),
        cost_estimate=pl.CostEstimate(
            flops=flops,
            transcendentals=tokens * heads * (mem + nrows),
            bytes_accessed=2 * (4 * tokens * width + mem * width + 4 * blocks * nrows * width)
            + 4 * mem * width,
        ),
    )(counts, near_rows, q, do, mk, *([kv_all] * (2 * NEAR)), zeros)


def shards(
    queries,
    key_states,
    value_states,
    out_grad,
    memory,
    near_device,
    near_slot,
    near_count,
    writer_block,
):
    seq_devices = lax.axis_size("seq")
    batch_devices = lax.axis_size("batch")
    my_index = lax.axis_index("seq")
    tokens = queries.shape[1]
    row_width = queries.shape[2]
    local_blocks = tokens // BLK
    rows_dev = MEM // seq_devices
    block_scale = 1.0 / math.sqrt(BLK)
    value_blocks = value_states[0].reshape(local_blocks, BLK, row_width)

    kv_all = lax.all_gather(
        jnp.concatenate([key_states[0], value_states[0]], axis=-1), "seq", axis=0, tiled=True
    )

    value_sums = jnp.sum(value_blocks, axis=1, dtype=jnp.float32)
    all_sums = lax.all_to_all(
        jnp.broadcast_to(value_sums[None], (seq_devices, local_blocks, row_width)),
        "seq",
        split_axis=0,
        concat_axis=0,
        tiled=True,
    ).reshape(seq_devices * local_blocks, row_width)
    memory_keys = (memory + jnp.take(all_sums, writer_block, axis=0) * block_scale).astype(
        jnp.bfloat16
    )
    near_block = (near_device * local_blocks + near_slot).astype(jnp.int32)
    my_near = lax.dynamic_slice_in_dim(near_block, my_index * local_blocks, local_blocks, 0).reshape(-1)
    my_count = lax.dynamic_slice_in_dim(near_count, my_index * local_blocks, local_blocks, 0)
    attended_rows, query_rows_grad, term, dkv = attention_core(
        my_count, my_near, queries[0], out_grad[0], memory_keys, kv_all
    )
    kv_grad = lax.psum_scatter(dkv, "seq", scatter_dimension=0, tiled=True)
    row_grads = lax.psum_scatter(
        term.astype(jnp.bfloat16), "seq", scatter_dimension=0, tiled=True
    ).astype(jnp.float32)
    my_writers = (
        lax.dynamic_slice_in_dim(writer_block, my_index * rows_dev, rows_dev, 0)
        - my_index * local_blocks
    )
    writer_match = (my_writers[:, None] == jnp.arange(local_blocks)[None, :])[:, :, None]
    spread = jnp.sum(jnp.where(writer_match, row_grads[:, None, :], 0.0), axis=0) * block_scale
    all_rows = lax.all_to_all(
        jnp.broadcast_to(row_grads[None], (batch_devices, rows_dev, row_width)),
        "batch",
        split_axis=0,
        concat_axis=0,
        tiled=True,
    )
    memory_grad = jnp.sum(all_rows, axis=0)
    value_sum = kv_grad[:, row_width:].astype(jnp.float32).reshape(local_blocks, BLK, row_width)
    attended = attended_rows.reshape(1, tokens, row_width)
    query_grad = query_rows_grad.reshape(1, tokens, row_width)
    key_grad = kv_grad[:, :row_width].reshape(1, tokens, row_width)
    value_grad = (value_sum + spread[:, None, :]).astype(jnp.bfloat16).reshape(1, tokens, row_width)
    return (attended, query_grad, key_grad, value_grad, memory_grad)


def solution(mesh):
    placed = (
        P("batch", "seq", None),
        P("batch", "seq", None),
        P("batch", "seq", None),
        P("batch", "seq", None),
        P(),
        P(),
        P(),
        P(),
        P(),
    )
    return jax.shard_map(
        shards,
        mesh=mesh,
        in_specs=placed,
        out_specs=(
            P("batch", "seq", None),
            P("batch", "seq", None),
            P("batch", "seq", None),
            P("batch", "seq", None),
            P("seq", None),
        ),
        check_vma=False,
    )
```

```python
import math

import jax
import jax.numpy as jnp
from jax import lax
from jax.experimental import pallas as pl
from jax.experimental.pallas import tpu as pltpu
from jax.sharding import PartitionSpec as P

HEADS = 8
HD = 128
BLK = 128
MEM = 1024
NEAR = 8


def _attn_body(cnt_ref, nb_ref, free_ref, q_ref, do_ref, mk_ref, *rest):
    k_refs = rest[:NEAR]
    v_refs = rest[NEAR : 2 * NEAR]
    o_ref, dq_ref, tm_ref, dkv_hbm, dks, dvs, sems, zero_strip, zero_sems = rest[2 * NEAR :]
    unnamed = zero_sems.shape[0]
    h = pl.program_id(0)
    n = pl.program_id(1)
    blocks = pl.num_programs(1)
    steps = pl.num_programs(0) * blocks
    step = h * blocks + n
    slot = step % 2
    heads = pl.num_programs(0)
    scale = 1.0 / math.sqrt(HD)
    f32 = jnp.float32
    nt = (((1,), (1,)), ((), ()))
    tn = (((0,), (0,)), ((), ()))
    def zero_copies():
        return [
            pltpu.make_async_copy(
                zero_strip,
                dkv_hbm.at[pl.ds(pl.multiple_of(free_ref[i] * BLK, BLK), BLK)],
                zero_sems.at[i],
            )
            for i in range(unnamed)
        ]

    @pl.when(step == 0)
    def _():
        zero_strip[...] = jnp.zeros(zero_strip.shape, zero_strip.dtype)
        for c in zero_copies():
            c.start()

    q = q_ref[...]
    do = do_ref[...]
    mk = mk_ref[...]
    nk = jnp.concatenate([r[...] for r in k_refs], axis=0)
    nv = jnp.concatenate([r[...] for r in v_refs], axis=0)
    sm = lax.dot_general(q, mk, nt, preferred_element_type=f32) * scale
    sn = lax.dot_general(q, nk, nt, preferred_element_type=f32) * scale
    col = lax.broadcasted_iota(jnp.int32, sn.shape, 1) // BLK
    sn = jnp.where(col < cnt_ref[n], sn, -jnp.inf)
    m = jnp.maximum(jnp.max(sm, axis=1, keepdims=True), jnp.max(sn, axis=1, keepdims=True))
    em = jnp.exp(sm - m)
    en = jnp.exp(sn - m)
    total = jnp.sum(em, axis=1, keepdims=True) + jnp.sum(en, axis=1, keepdims=True)
    pm = em / total
    pn = en / total
    wm = pm.astype(jnp.bfloat16)
    wn = pn.astype(jnp.bfloat16)
    o = (
        jnp.dot(wm, mk, preferred_element_type=f32) + jnp.dot(wn, nv, preferred_element_type=f32)
    ).astype(jnp.bfloat16)
    o_ref[...] = o
    gd = jnp.sum(do.astype(f32) * o.astype(f32), axis=1, keepdims=True)
    dpm = lax.dot_general(do, mk, nt, preferred_element_type=f32)
    dpn = lax.dot_general(do, nv, nt, preferred_element_type=f32)
    dsm = (pm * (dpm - gd)).astype(jnp.bfloat16)
    dsn = (pn * (dpn - gd)).astype(jnp.bfloat16)
    dq_ref[...] = (
        (jnp.dot(dsm, mk, preferred_element_type=f32) + jnp.dot(dsn, nk, preferred_element_type=f32))
        * scale
    ).astype(jnp.bfloat16)
    dk = (lax.dot_general(dsn, q, tn, preferred_element_type=f32) * scale).astype(jnp.bfloat16)
    dv = lax.dot_general(wn, do, tn, preferred_element_type=f32).astype(jnp.bfloat16)
    tm = lax.dot_general(dsm, q, tn, preferred_element_type=f32) * scale + lax.dot_general(
        wm, do, tn, preferred_element_type=f32
    )

    @pl.when(n == 0)
    def _():
        tm_ref[...] = tm

    @pl.when(n != 0)
    def _():
        tm_ref[...] += tm

    def copies(at_step, at_slot):
        at_h = at_step // blocks
        at_n = at_step % blocks
        out = []
        for j in range(NEAR):
            rows = pl.ds(pl.multiple_of(nb_ref[at_n * NEAR + j] * BLK, BLK), BLK)
            out.append(
                pltpu.make_async_copy(
                    dks.at[at_slot, j],
                    dkv_hbm.at[rows, pl.ds(pl.multiple_of(at_h * HD, HD), HD)],
                    sems.at[at_slot, j],
                )
            )
            out.append(
                pltpu.make_async_copy(
                    dvs.at[at_slot, j],
                    dkv_hbm.at[rows, pl.ds(pl.multiple_of((heads + at_h) * HD, HD), HD)],
                    sems.at[at_slot, NEAR + j],
                )
            )
        return out

    @pl.when(step >= 2)
    def _():
        for c in copies(step - 2, slot):
            c.wait()

    for j in range(NEAR):
        dks[slot, j] = dk[j * BLK : (j + 1) * BLK]
        dvs[slot, j] = dv[j * BLK : (j + 1) * BLK]
    for c in copies(step, slot):
        c.start()

    @pl.when(step == steps - 1)
    def _():
        for c in copies(step - 1, 1 - slot):
            c.wait()
        for c in copies(step, slot):
            c.wait()
        for c in zero_copies():
            c.wait()


def attention_core(counts, near_rows, free_rows, q, do, mk, kv_all):
    tokens, width = q.shape
    blocks = tokens // BLK
    mem = mk.shape[0]
    heads = width // HD
    nrows = NEAR * BLK
    qspec = pl.BlockSpec((BLK, HD), lambda h, n, c, t, f: (n, h))
    mspec = pl.BlockSpec((mem, HD), lambda h, n, c, t, f: (0, h))

    def kv_spec(j, which):
        return pl.BlockSpec((BLK, HD), lambda h, n, c, t, f: (t[n * NEAR + j], which * heads + h))

    anyspec = pl.BlockSpec(memory_space=pl.ANY)
    flops = 2 * tokens * width * (mem + nrows) * 4 + 2 * tokens * width * (nrows * 2 + mem * 2)
    grid_spec = pltpu.PrefetchScalarGridSpec(
        num_scalar_prefetch=3,
        grid=(heads, blocks),
        in_specs=[qspec, qspec, mspec]
        + [kv_spec(j, 0) for j in range(NEAR)]
        + [kv_spec(j, 1) for j in range(NEAR)],
        out_specs=[qspec, qspec, mspec, anyspec],
        scratch_shapes=[
            pltpu.VMEM((2, NEAR, BLK, HD), jnp.bfloat16),
            pltpu.VMEM((2, NEAR, BLK, HD), jnp.bfloat16),
            pltpu.SemaphoreType.DMA((2, 2 * NEAR)),
            pltpu.VMEM((BLK, kv_all.shape[1]), jnp.bfloat16),
            pltpu.SemaphoreType.DMA((free_rows.shape[0],)),
        ],
    )
    return pl.pallas_call(
        _attn_body,
        grid_spec=grid_spec,
        out_shape=[
            jax.ShapeDtypeStruct((tokens, width), jnp.bfloat16),
            jax.ShapeDtypeStruct((tokens, width), jnp.bfloat16),
            jax.ShapeDtypeStruct((mem, width), jnp.float32),
            jax.ShapeDtypeStruct(kv_all.shape, jnp.bfloat16),
        ],
        compiler_params=pltpu.CompilerParams(dimension_semantics=("arbitrary", "arbitrary")),
        cost_estimate=pl.CostEstimate(
            flops=flops,
            transcendentals=tokens * heads * (mem + nrows),
            bytes_accessed=2 * (4 * tokens * width + mem * width + 4 * blocks * nrows * width)
            + 4 * mem * width,
        ),
    )(counts, near_rows, free_rows, q, do, mk, *([kv_all] * (2 * NEAR)))


def shards(
    queries,
    key_states,
    value_states,
    out_grad,
    memory,
    near_device,
    near_slot,
    near_count,
    writer_block,
):
    seq_devices = lax.axis_size("seq")
    batch_devices = lax.axis_size("batch")
    my_index = lax.axis_index("seq")
    tokens = queries.shape[1]
    row_width = queries.shape[2]
    local_blocks = tokens // BLK
    rows_dev = MEM // seq_devices
    block_scale = 1.0 / math.sqrt(BLK)
    value_blocks = value_states[0].reshape(local_blocks, BLK, row_width)

    kv_all = lax.all_gather(
        jnp.concatenate([key_states[0], value_states[0]], axis=-1), "seq", axis=0, tiled=True
    )

    value_sums = jnp.sum(value_blocks, axis=1, dtype=jnp.float32)
    all_sums = lax.all_to_all(
        jnp.broadcast_to(value_sums[None], (seq_devices, local_blocks, row_width)),
        "seq",
        split_axis=0,
        concat_axis=0,
        tiled=True,
    ).reshape(seq_devices * local_blocks, row_width)
    memory_keys = (memory + jnp.take(all_sums, writer_block, axis=0) * block_scale).astype(
        jnp.bfloat16
    )
    near_block = (near_device * local_blocks + near_slot).astype(jnp.int32)
    my_near = lax.dynamic_slice_in_dim(near_block, my_index * local_blocks, local_blocks, 0).reshape(-1)
    my_count = lax.dynamic_slice_in_dim(near_count, my_index * local_blocks, local_blocks, 0)
    all_blocks = seq_devices * local_blocks
    named = jnp.any(my_near[None, :] == jnp.arange(all_blocks)[:, None], axis=1)
    free_rows = jnp.argsort(named.astype(jnp.int32), stable=True)[: all_blocks - my_near.shape[0]]
    free_rows = free_rows.astype(jnp.int32)
    attended_rows, query_rows_grad, term, dkv = attention_core(
        my_count, my_near, free_rows, queries[0], out_grad[0], memory_keys, kv_all
    )
    kv_grad = lax.psum_scatter(dkv, "seq", scatter_dimension=0, tiled=True)
    row_parts = lax.all_to_all(
        term.astype(jnp.bfloat16).reshape(seq_devices, rows_dev, row_width),
        "seq",
        split_axis=0,
        concat_axis=0,
        tiled=True,
    )
    row_grads = jnp.sum(row_parts.astype(jnp.float32), axis=0)
    my_writers = (
        lax.dynamic_slice_in_dim(writer_block, my_index * rows_dev, rows_dev, 0)
        - my_index * local_blocks
    )
    writer_match = (my_writers[:, None] == jnp.arange(local_blocks)[None, :])[:, :, None]
    spread = jnp.sum(jnp.where(writer_match, row_grads[:, None, :], 0.0), axis=0) * block_scale
    all_rows = lax.all_to_all(
        jnp.broadcast_to(row_grads[None], (batch_devices, rows_dev, row_width)),
        "batch",
        split_axis=0,
        concat_axis=0,
        tiled=True,
    )
    memory_grad = jnp.sum(all_rows, axis=0)
    value_sum = kv_grad[:, row_width:].astype(jnp.float32).reshape(local_blocks, BLK, row_width)
    attended = attended_rows.reshape(1, tokens, row_width)
    query_grad = query_rows_grad.reshape(1, tokens, row_width)
    key_grad = kv_grad[:, :row_width].reshape(1, tokens, row_width)
    value_grad = (value_sum + spread[:, None, :]).astype(jnp.bfloat16).reshape(1, tokens, row_width)
    return (attended, query_grad, key_grad, value_grad, memory_grad)


def solution(mesh):
    placed = (
        P("batch", "seq", None),
        P("batch", "seq", None),
        P("batch", "seq", None),
        P("batch", "seq", None),
        P(),
        P(),
        P(),
        P(),
        P(),
    )
    return jax.shard_map(
        shards,
        mesh=mesh,
        in_specs=placed,
        out_specs=(
            P("batch", "seq", None),
            P("batch", "seq", None),
            P("batch", "seq", None),
            P("batch", "seq", None),
            P("seq", None),
        ),
        check_vma=False,
    )
```

```python
import math

import jax
import jax.numpy as jnp
from jax import lax
from jax.experimental import pallas as pl
from jax.experimental.pallas import tpu as pltpu
from jax.sharding import PartitionSpec as P

HEADS = 8
HD = 128
BLK = 128
MEM = 1024
NEAR = 8


def _rows_of(col):
    eye = lax.broadcasted_iota(jnp.int32, (BLK, BLK), 0) == lax.broadcasted_iota(jnp.int32, (BLK, BLK), 1)
    return jnp.sum(jnp.where(eye, col, 0.0), axis=0, keepdims=True)


def _query_body(cnt_ref, nb_ref, q_ref, do_ref, mk_ref, *rest):
    k_refs = rest[:NEAR]
    v_refs = rest[NEAR : 2 * NEAR]
    o_ref, dq_ref, tm_ref, st_ref = rest[2 * NEAR :]
    n = pl.program_id(0)
    h = pl.program_id(1)
    heads = pl.num_programs(1)
    scale = 1.0 / math.sqrt(HD)
    f32 = jnp.float32
    nt = (((1,), (1,)), ((), ()))
    tn = (((0,), (0,)), ((), ()))
    q = q_ref[...]
    do = do_ref[...]
    mk = mk_ref[...]
    nk = jnp.concatenate([r[...] for r in k_refs], axis=0)
    nv = jnp.concatenate([r[...] for r in v_refs], axis=0)
    sm = lax.dot_general(q, mk, nt, preferred_element_type=f32) * scale
    sn = lax.dot_general(q, nk, nt, preferred_element_type=f32) * scale
    col = lax.broadcasted_iota(jnp.int32, sn.shape, 1) // BLK
    sn = jnp.where(col < cnt_ref[n], sn, -jnp.inf)
    m = jnp.maximum(jnp.max(sm, axis=1, keepdims=True), jnp.max(sn, axis=1, keepdims=True))
    em = jnp.exp(sm - m)
    en = jnp.exp(sn - m)
    total = jnp.sum(em, axis=1, keepdims=True) + jnp.sum(en, axis=1, keepdims=True)
    pm = em / total
    pn = en / total
    wm = pm.astype(jnp.bfloat16)
    wn = pn.astype(jnp.bfloat16)
    o = (
        jnp.dot(wm, mk, preferred_element_type=f32) + jnp.dot(wn, nv, preferred_element_type=f32)
    ).astype(jnp.bfloat16)
    o_ref[...] = o
    gd = jnp.sum(do.astype(f32) * o.astype(f32), axis=1, keepdims=True)
    dpm = lax.dot_general(do, mk, nt, preferred_element_type=f32)
    dpn = lax.dot_general(do, nv, nt, preferred_element_type=f32)
    dsm = (pm * (dpm - gd)).astype(jnp.bfloat16)
    dsn = (pn * (dpn - gd)).astype(jnp.bfloat16)
    dq_ref[...] = (
        (jnp.dot(dsm, mk, preferred_element_type=f32) + jnp.dot(dsn, nk, preferred_element_type=f32))
        * scale
    ).astype(jnp.bfloat16)
    tm_ref[0] = lax.dot_general(dsm, q, tn, preferred_element_type=f32) * scale + lax.dot_general(
        wm, do, tn, preferred_element_type=f32
    )
    st_ref[pl.ds(h, 1), :] = _rows_of(m)
    st_ref[pl.ds(heads + h, 1), :] = _rows_of(total)
    st_ref[pl.ds(2 * heads + h, 1), :] = _rows_of(gd)


def query_core(counts, near_rows, q, do, mk, kv_all):
    tokens, width = q.shape
    blocks = tokens // BLK
    mem = mk.shape[0]
    heads = width // HD
    nrows = NEAR * BLK
    qspec = pl.BlockSpec((BLK, HD), lambda n, h, c, t: (n, h))
    mspec = pl.BlockSpec((mem, HD), lambda n, h, c, t: (0, h))

    def kv_spec(j, which):
        return pl.BlockSpec((BLK, HD), lambda n, h, c, t: (t[n * NEAR + j], which * heads + h))

    flops = 2 * tokens * width * (mem + nrows) * 4 + 2 * tokens * width * (nrows + mem * 2)
    grid_spec = pltpu.PrefetchScalarGridSpec(
        num_scalar_prefetch=2,
        grid=(blocks, heads),
        in_specs=[qspec, qspec, mspec]
        + [kv_spec(j, 0) for j in range(NEAR)]
        + [kv_spec(j, 1) for j in range(NEAR)],
        out_specs=[
            qspec,
            qspec,
            pl.BlockSpec((1, mem, HD), lambda n, h, c, t: (n, 0, h)),
            pl.BlockSpec((3 * heads, BLK), lambda n, h, c, t: (0, n)),
        ],
    )
    return pl.pallas_call(
        _query_body,
        grid_spec=grid_spec,
        out_shape=[
            jax.ShapeDtypeStruct((tokens, width), jnp.bfloat16),
            jax.ShapeDtypeStruct((tokens, width), jnp.bfloat16),
            jax.ShapeDtypeStruct((blocks, mem, width), jnp.float32),
            jax.ShapeDtypeStruct((3 * heads, tokens), jnp.float32),
        ],
        compiler_params=pltpu.CompilerParams(dimension_semantics=("arbitrary", "arbitrary")),
        cost_estimate=pl.CostEstimate(
            flops=flops,
            transcendentals=tokens * heads * (mem + nrows),
            bytes_accessed=2 * (4 * tokens * width + blocks * mem * width + 2 * blocks * nrows * width)
            + 4 * blocks * mem * width,
        ),
    )(counts, near_rows, q, do, mk, *([kv_all] * (2 * NEAR)))


def _owner_body(src_blk, src_slot, src_live, my_slot, qd_ref, st_ref, k_ref, v_ref, dk_ref, dv_ref):
    s = pl.program_id(0)
    heads = k_ref.shape[1] // HD
    scale = 1.0 / math.sqrt(HD)
    f32 = jnp.float32
    nt = (((1,), (1,)), ((), ()))

    @pl.when(s == 0)
    def _():
        dk_ref[...] = jnp.zeros(dk_ref.shape, f32)
        dv_ref[...] = jnp.zeros(dv_ref.shape, f32)

    @pl.when(src_live[s] != 0)
    def _():
        rows = pl.ds(pl.multiple_of(my_slot[s] * BLK, BLK), BLK)
        st = st_ref[0]
        for h in range(heads):
            cols = pl.ds(h * HD, HD)
            q_h = qd_ref[:, cols]
            do_h = qd_ref[:, pl.ds((heads + h) * HD, HD)]
            k_h = k_ref[rows, cols]
            v_h = v_ref[rows, cols]
            row_max = st[h : h + 1]
            row_total = st[heads + h : heads + h + 1]
            grad_dot = st[2 * heads + h : 2 * heads + h + 1]
            score_t = lax.dot_general(k_h, q_h, nt, preferred_element_type=f32) * scale
            prob_t = jnp.exp(score_t - row_max) / row_total
            weight_t = prob_t.astype(jnp.bfloat16)
            dprob_t = lax.dot_general(v_h, do_h, nt, preferred_element_type=f32)
            dscore_t = (prob_t * (dprob_t - grad_dot)).astype(jnp.bfloat16)
            dk = (jnp.dot(dscore_t, q_h, preferred_element_type=f32) * scale).astype(jnp.bfloat16)
            dv = jnp.dot(weight_t, do_h, preferred_element_type=f32).astype(jnp.bfloat16)
            dk_ref[rows, cols] += dk.astype(f32)
            dv_ref[rows, cols] += dv.astype(f32)


def owner_core(src_blk, src_slot, src_live, my_slot, qd_all, stats_all, k_loc, v_loc):
    sources = src_blk.shape[0]
    tokens, width = k_loc.shape
    full = pl.BlockSpec((tokens, width), lambda s, a, b, c, d: (0, 0))
    grid_spec = pltpu.PrefetchScalarGridSpec(
        num_scalar_prefetch=4,
        grid=(sources,),
        in_specs=[
            pl.BlockSpec((BLK, 2 * width), lambda s, a, b, c, d: (a[s], 0)),
            pl.BlockSpec((1, stats_all.shape[1], BLK), lambda s, a, b, c, d: (s, 0, b[s])),
            full,
            full,
        ],
        out_specs=[full, full],
    )
    return pl.pallas_call(
        _owner_body,
        grid_spec=grid_spec,
        out_shape=[
            jax.ShapeDtypeStruct((tokens, width), jnp.float32),
            jax.ShapeDtypeStruct((tokens, width), jnp.float32),
        ],
        compiler_params=pltpu.CompilerParams(dimension_semantics=("arbitrary",)),
        cost_estimate=pl.CostEstimate(
            flops=sources * 8 * BLK * BLK * width,
            transcendentals=sources * BLK * BLK * (width // HD),
            bytes_accessed=sources * BLK * 2 * width * 2 + 2 * tokens * width * (2 + 8),
        ),
    )(src_blk, src_slot, src_live, my_slot, qd_all, stats_all, k_loc, v_loc)


def shards(
    queries,
    key_states,
    value_states,
    out_grad,
    memory,
    near_device,
    near_slot,
    near_count,
    writer_block,
):
    seq_devices = lax.axis_size("seq")
    batch_devices = lax.axis_size("batch")
    my_index = lax.axis_index("seq")
    tokens = queries.shape[1]
    row_width = queries.shape[2]
    local_blocks = tokens // BLK
    rows_dev = MEM // seq_devices
    block_scale = 1.0 / math.sqrt(BLK)
    value_blocks = value_states[0].reshape(local_blocks, BLK, row_width)

    kv_all = lax.all_gather(
        jnp.concatenate([key_states[0], value_states[0]], axis=-1), "seq", axis=0, tiled=True
    )

    value_sums = jnp.sum(value_blocks, axis=1, dtype=jnp.float32)
    all_sums = lax.all_to_all(
        jnp.broadcast_to(value_sums[None], (seq_devices, local_blocks, row_width)),
        "seq",
        split_axis=0,
        concat_axis=0,
        tiled=True,
    ).reshape(seq_devices * local_blocks, row_width)
    memory_keys = (memory + jnp.take(all_sums, writer_block, axis=0) * block_scale).astype(
        jnp.bfloat16
    )
    near_block = (near_device * local_blocks + near_slot).astype(jnp.int32)
    my_near = lax.dynamic_slice_in_dim(near_block, my_index * local_blocks, local_blocks, 0).reshape(-1)
    my_count = lax.dynamic_slice_in_dim(near_count, my_index * local_blocks, local_blocks, 0)
    qd_all = lax.all_gather(
        jnp.concatenate([queries[0], out_grad[0]], axis=-1), "seq", axis=0, tiled=True
    )
    attended_rows, query_rows_grad, term, stats = query_core(
        my_count, my_near, queries[0], out_grad[0], memory_keys, kv_all
    )
    stats_all = lax.all_to_all(
        jnp.broadcast_to(stats[None], (seq_devices,) + stats.shape),
        "seq",
        split_axis=0,
        concat_axis=0,
        tiled=True,
    )
    row_parts = lax.all_to_all(
        jnp.sum(term, axis=0).astype(jnp.bfloat16).reshape(seq_devices, rows_dev, row_width),
        "seq",
        split_axis=0,
        concat_axis=0,
        tiled=True,
    )
    row_grads = jnp.sum(row_parts.astype(jnp.float32), axis=0)
    near_width = near_device.shape[1]
    entries = local_blocks * near_width
    target = near_device.reshape(seq_devices, entries)
    source_slot = near_slot.reshape(seq_devices, entries)
    live = (
        jnp.arange(near_width)[None, None, :]
        < near_count.reshape(seq_devices, local_blocks)[:, :, None]
    ).reshape(seq_devices, entries)
    names_me = target == my_index
    entry_at = jnp.argmax(names_me, axis=1).astype(jnp.int32)
    src_slot = entry_at // near_width
    src_blk = (jnp.arange(seq_devices, dtype=jnp.int32) * local_blocks + src_slot).astype(jnp.int32)
    src_live = jnp.any(names_me & live, axis=1).astype(jnp.int32)
    my_slot = jnp.sum(jnp.where(names_me, source_slot, 0), axis=1).astype(jnp.int32)
    dk_sum, dv_sum = owner_core(
        src_blk, src_slot, src_live, my_slot, qd_all, stats_all, key_states[0], value_states[0]
    )
    my_writers = (
        lax.dynamic_slice_in_dim(writer_block, my_index * rows_dev, rows_dev, 0)
        - my_index * local_blocks
    )
    writer_match = (my_writers[:, None] == jnp.arange(local_blocks)[None, :])[:, :, None]
    spread = jnp.sum(jnp.where(writer_match, row_grads[:, None, :], 0.0), axis=0) * block_scale
    all_rows = lax.all_to_all(
        jnp.broadcast_to(row_grads[None], (batch_devices, rows_dev, row_width)),
        "batch",
        split_axis=0,
        concat_axis=0,
        tiled=True,
    )
    memory_grad = jnp.sum(all_rows, axis=0)
    value_sum = dv_sum.reshape(local_blocks, BLK, row_width)
    attended = attended_rows.reshape(1, tokens, row_width)
    query_grad = query_rows_grad.reshape(1, tokens, row_width)
    key_grad = dk_sum.astype(jnp.bfloat16).reshape(1, tokens, row_width)
    value_grad = (value_sum + spread[:, None, :]).astype(jnp.bfloat16).reshape(1, tokens, row_width)
    return (attended, query_grad, key_grad, value_grad, memory_grad)


def solution(mesh):
    placed = (
        P("batch", "seq", None),
        P("batch", "seq", None),
        P("batch", "seq", None),
        P("batch", "seq", None),
        P(),
        P(),
        P(),
        P(),
        P(),
    )
    return jax.shard_map(
        shards,
        mesh=mesh,
        in_specs=placed,
        out_specs=(
            P("batch", "seq", None),
            P("batch", "seq", None),
            P("batch", "seq", None),
            P("batch", "seq", None),
            P("seq", None),
        ),
        check_vma=False,
    )
```

```python
import functools
import math

import jax
import jax.numpy as jnp
from jax import lax
from jax.experimental import pallas as pl
from jax.experimental.pallas import tpu as pltpu
from jax.sharding import PartitionSpec as P

HEADS = 8
HD = 128
BLK = 128
MEM = 1024
NEAR = 8


def _rows_of(col):
    eye = lax.broadcasted_iota(jnp.int32, (BLK, BLK), 0) == lax.broadcasted_iota(jnp.int32, (BLK, BLK), 1)
    return jnp.sum(jnp.where(eye, col, 0.0), axis=0, keepdims=True)


def _query_body(cnt_ref, nb_ref, q_ref, do_ref, mk_ref, *rest):
    k_refs = rest[:NEAR]
    v_refs = rest[NEAR : 2 * NEAR]
    o_ref, dq_ref, tm_ref, st_ref = rest[2 * NEAR :]
    n = pl.program_id(0)
    h = pl.program_id(1)
    heads = pl.num_programs(1)
    scale = 1.0 / math.sqrt(HD)
    f32 = jnp.float32
    nt = (((1,), (1,)), ((), ()))
    tn = (((0,), (0,)), ((), ()))
    q = q_ref[...]
    do = do_ref[...]
    mk = mk_ref[...]
    nk = jnp.concatenate([r[...] for r in k_refs], axis=0)
    nv = jnp.concatenate([r[...] for r in v_refs], axis=0)
    sm = lax.dot_general(q, mk, nt, preferred_element_type=f32) * scale
    sn = lax.dot_general(q, nk, nt, preferred_element_type=f32) * scale
    col = lax.broadcasted_iota(jnp.int32, sn.shape, 1) // BLK
    sn = jnp.where(col < cnt_ref[n], sn, -jnp.inf)
    m = jnp.maximum(jnp.max(sm, axis=1, keepdims=True), jnp.max(sn, axis=1, keepdims=True))
    em = jnp.exp(sm - m)
    en = jnp.exp(sn - m)
    total = jnp.sum(em, axis=1, keepdims=True) + jnp.sum(en, axis=1, keepdims=True)
    pm = em / total
    pn = en / total
    wm = pm.astype(jnp.bfloat16)
    wn = pn.astype(jnp.bfloat16)
    o = (
        jnp.dot(wm, mk, preferred_element_type=f32) + jnp.dot(wn, nv, preferred_element_type=f32)
    ).astype(jnp.bfloat16)
    o_ref[...] = o
    gd = jnp.sum(do.astype(f32) * o.astype(f32), axis=1, keepdims=True)
    dpm = lax.dot_general(do, mk, nt, preferred_element_type=f32)
    dpn = lax.dot_general(do, nv, nt, preferred_element_type=f32)
    dsm = (pm * (dpm - gd)).astype(jnp.bfloat16)
    dsn = (pn * (dpn - gd)).astype(jnp.bfloat16)
    dq_ref[...] = (
        (jnp.dot(dsm, mk, preferred_element_type=f32) + jnp.dot(dsn, nk, preferred_element_type=f32))
        * scale
    ).astype(jnp.bfloat16)
    tm_ref[0] = lax.dot_general(dsm, q, tn, preferred_element_type=f32) * scale + lax.dot_general(
        wm, do, tn, preferred_element_type=f32
    )
    st_ref[pl.ds(h, 1), :] = _rows_of(m)
    st_ref[pl.ds(heads + h, 1), :] = _rows_of(total)
    st_ref[pl.ds(2 * heads + h, 1), :] = _rows_of(gd)


def query_core(counts, near_rows, q, do, mk, kv_all):
    tokens, width = q.shape
    blocks = tokens // BLK
    mem = mk.shape[0]
    heads = width // HD
    nrows = NEAR * BLK
    qspec = pl.BlockSpec((BLK, HD), lambda n, h, c, t: (n, h))
    mspec = pl.BlockSpec((mem, HD), lambda n, h, c, t: (0, h))

    def kv_spec(j, which):
        return pl.BlockSpec((BLK, HD), lambda n, h, c, t: (t[n * NEAR + j], which * heads + h))

    flops = 2 * tokens * width * (mem + nrows) * 4 + 2 * tokens * width * (nrows + mem * 2)
    grid_spec = pltpu.PrefetchScalarGridSpec(
        num_scalar_prefetch=2,
        grid=(blocks, heads),
        in_specs=[qspec, qspec, mspec]
        + [kv_spec(j, 0) for j in range(NEAR)]
        + [kv_spec(j, 1) for j in range(NEAR)],
        out_specs=[
            qspec,
            qspec,
            pl.BlockSpec((1, mem, HD), lambda n, h, c, t: (n, 0, h)),
            pl.BlockSpec((3 * heads, BLK), lambda n, h, c, t: (0, n)),
        ],
    )
    return pl.pallas_call(
        _query_body,
        grid_spec=grid_spec,
        out_shape=[
            jax.ShapeDtypeStruct((tokens, width), jnp.bfloat16),
            jax.ShapeDtypeStruct((tokens, width), jnp.bfloat16),
            jax.ShapeDtypeStruct((blocks, mem, width), jnp.float32),
            jax.ShapeDtypeStruct((3 * heads, tokens), jnp.float32),
        ],
        compiler_params=pltpu.CompilerParams(dimension_semantics=("arbitrary", "arbitrary")),
        cost_estimate=pl.CostEstimate(
            flops=flops,
            transcendentals=tokens * heads * (mem + nrows),
            bytes_accessed=2 * (4 * tokens * width + blocks * mem * width + 2 * blocks * nrows * width)
            + 4 * blocks * mem * width,
        ),
    )(counts, near_rows, q, do, mk, *([kv_all] * (2 * NEAR)))


def _owner_body(head_base, group_heads, src_blk, src_slot, src_live, my_slot, qd_ref, st_ref, k_ref, v_ref, dk_ref, dv_ref):
    s = pl.program_id(0)
    heads = k_ref.shape[1] // HD
    scale = 1.0 / math.sqrt(HD)
    f32 = jnp.float32
    nt = (((1,), (1,)), ((), ()))

    @pl.when(s == 0)
    def _():
        dk_ref[...] = jnp.zeros(dk_ref.shape, f32)
        dv_ref[...] = jnp.zeros(dv_ref.shape, f32)

    @pl.when(src_live[s] != 0)
    def _():
        rows = pl.ds(pl.multiple_of(my_slot[s] * BLK, BLK), BLK)
        st = st_ref[0]
        for h in range(group_heads):
            hh = head_base + h
            cols = pl.ds(h * HD, HD)
            q_h = qd_ref[:, cols]
            do_h = qd_ref[:, pl.ds((group_heads + h) * HD, HD)]
            k_h = k_ref[rows, pl.ds(hh * HD, HD)]
            v_h = v_ref[rows, pl.ds(hh * HD, HD)]
            row_max = st[hh : hh + 1]
            row_total = st[heads + hh : heads + hh + 1]
            grad_dot = st[2 * heads + hh : 2 * heads + hh + 1]
            score_t = lax.dot_general(k_h, q_h, nt, preferred_element_type=f32) * scale
            prob_t = jnp.exp(score_t - row_max) / row_total
            weight_t = prob_t.astype(jnp.bfloat16)
            dprob_t = lax.dot_general(v_h, do_h, nt, preferred_element_type=f32)
            dscore_t = (prob_t * (dprob_t - grad_dot)).astype(jnp.bfloat16)
            dk = (jnp.dot(dscore_t, q_h, preferred_element_type=f32) * scale).astype(jnp.bfloat16)
            dv = jnp.dot(weight_t, do_h, preferred_element_type=f32).astype(jnp.bfloat16)
            dk_ref[rows, cols] += dk.astype(f32)
            dv_ref[rows, cols] += dv.astype(f32)


def owner_core(src_blk, src_slot, src_live, my_slot, qd_all, stats_all, k_loc, v_loc, head_base):
    sources = src_blk.shape[0]
    tokens, full_width = k_loc.shape
    width = qd_all.shape[1] // 2
    full = pl.BlockSpec((tokens, full_width), lambda s, a, b, c, d: (0, 0))
    part = pl.BlockSpec((tokens, width), lambda s, a, b, c, d: (0, 0))
    grid_spec = pltpu.PrefetchScalarGridSpec(
        num_scalar_prefetch=4,
        grid=(sources,),
        in_specs=[
            pl.BlockSpec((BLK, 2 * width), lambda s, a, b, c, d: (a[s], 0)),
            pl.BlockSpec((1, stats_all.shape[1], BLK), lambda s, a, b, c, d: (s, 0, b[s])),
            full,
            full,
        ],
        out_specs=[part, part],
    )
    return pl.pallas_call(
        functools.partial(_owner_body, head_base, width // HD),
        grid_spec=grid_spec,
        out_shape=[
            jax.ShapeDtypeStruct((tokens, width), jnp.float32),
            jax.ShapeDtypeStruct((tokens, width), jnp.float32),
        ],
        compiler_params=pltpu.CompilerParams(dimension_semantics=("arbitrary",)),
        cost_estimate=pl.CostEstimate(
            flops=sources * 8 * BLK * BLK * width,
            transcendentals=sources * BLK * BLK * (width // HD),
            bytes_accessed=sources * BLK * 2 * width * 2 + 2 * tokens * width * (2 + 8),
        ),
    )(src_blk, src_slot, src_live, my_slot, qd_all, stats_all, k_loc, v_loc)


def shards(
    queries,
    key_states,
    value_states,
    out_grad,
    memory,
    near_device,
    near_slot,
    near_count,
    writer_block,
):
    seq_devices = lax.axis_size("seq")
    batch_devices = lax.axis_size("batch")
    my_index = lax.axis_index("seq")
    tokens = queries.shape[1]
    row_width = queries.shape[2]
    local_blocks = tokens // BLK
    rows_dev = MEM // seq_devices
    block_scale = 1.0 / math.sqrt(BLK)
    value_blocks = value_states[0].reshape(local_blocks, BLK, row_width)

    kv_all = lax.all_gather(
        jnp.concatenate([key_states[0], value_states[0]], axis=-1), "seq", axis=0, tiled=True
    )

    value_sums = jnp.sum(value_blocks, axis=1, dtype=jnp.float32)
    all_sums = lax.all_to_all(
        jnp.broadcast_to(value_sums[None], (seq_devices, local_blocks, row_width)),
        "seq",
        split_axis=0,
        concat_axis=0,
        tiled=True,
    ).reshape(seq_devices * local_blocks, row_width)
    memory_keys = (memory + jnp.take(all_sums, writer_block, axis=0) * block_scale).astype(
        jnp.bfloat16
    )
    near_block = (near_device * local_blocks + near_slot).astype(jnp.int32)
    my_near = lax.dynamic_slice_in_dim(near_block, my_index * local_blocks, local_blocks, 0).reshape(-1)
    my_count = lax.dynamic_slice_in_dim(near_count, my_index * local_blocks, local_blocks, 0)
    half = row_width // 2
    qd_lo = lax.all_gather(
        jnp.concatenate([queries[0][:, :half], out_grad[0][:, :half]], axis=-1), "seq", axis=0, tiled=True
    )
    qd_hi = lax.all_gather(
        jnp.concatenate([queries[0][:, half:], out_grad[0][:, half:]], axis=-1), "seq", axis=0, tiled=True
    )
    attended_rows, query_rows_grad, term, stats = query_core(
        my_count, my_near, queries[0], out_grad[0], memory_keys, kv_all
    )
    stats_all = lax.all_to_all(
        jnp.broadcast_to(stats[None], (seq_devices,) + stats.shape),
        "seq",
        split_axis=0,
        concat_axis=0,
        tiled=True,
    )
    row_parts = lax.all_to_all(
        jnp.sum(term, axis=0).astype(jnp.bfloat16).reshape(seq_devices, rows_dev, row_width),
        "seq",
        split_axis=0,
        concat_axis=0,
        tiled=True,
    )
    row_grads = jnp.sum(row_parts.astype(jnp.float32), axis=0)
    near_width = near_device.shape[1]
    entries = local_blocks * near_width
    target = near_device.reshape(seq_devices, entries)
    source_slot = near_slot.reshape(seq_devices, entries)
    live = (
        jnp.arange(near_width)[None, None, :]
        < near_count.reshape(seq_devices, local_blocks)[:, :, None]
    ).reshape(seq_devices, entries)
    names_me = target == my_index
    entry_at = jnp.argmax(names_me, axis=1).astype(jnp.int32)
    src_slot = entry_at // near_width
    src_blk = (jnp.arange(seq_devices, dtype=jnp.int32) * local_blocks + src_slot).astype(jnp.int32)
    src_live = jnp.any(names_me & live, axis=1).astype(jnp.int32)
    my_slot = jnp.sum(jnp.where(names_me, source_slot, 0), axis=1).astype(jnp.int32)
    dk_lo, dv_lo = owner_core(
        src_blk, src_slot, src_live, my_slot, qd_lo, stats_all, key_states[0], value_states[0], 0
    )
    my_writers = (
        lax.dynamic_slice_in_dim(writer_block, my_index * rows_dev, rows_dev, 0)
        - my_index * local_blocks
    )
    writer_match = (my_writers[:, None] == jnp.arange(local_blocks)[None, :])[:, :, None]
    spread = jnp.sum(jnp.where(writer_match, row_grads[:, None, :], 0.0), axis=0) * block_scale
    all_rows = lax.all_to_all(
        jnp.broadcast_to(row_grads[None], (batch_devices, rows_dev, row_width)),
        "batch",
        split_axis=0,
        concat_axis=0,
        tiled=True,
    )
    memory_grad = jnp.sum(all_rows, axis=0)
    memory_grad, qd_hi = lax.optimization_barrier((memory_grad, qd_hi))
    dk_hi, dv_hi = owner_core(
        src_blk, src_slot, src_live, my_slot, qd_hi, stats_all, key_states[0], value_states[0],
        half // HD,
    )
    dk_sum = jnp.concatenate([dk_lo, dk_hi], axis=-1)
    dv_sum = jnp.concatenate([dv_lo, dv_hi], axis=-1)
    value_sum = dv_sum.reshape(local_blocks, BLK, row_width)
    attended = attended_rows.reshape(1, tokens, row_width)
    query_grad = query_rows_grad.reshape(1, tokens, row_width)
    key_grad = dk_sum.astype(jnp.bfloat16).reshape(1, tokens, row_width)
    value_grad = (value_sum + spread[:, None, :]).astype(jnp.bfloat16).reshape(1, tokens, row_width)
    return (attended, query_grad, key_grad, value_grad, memory_grad)


def solution(mesh):
    placed = (
        P("batch", "seq", None),
        P("batch", "seq", None),
        P("batch", "seq", None),
        P("batch", "seq", None),
        P(),
        P(),
        P(),
        P(),
        P(),
    )
    return jax.shard_map(
        shards,
        mesh=mesh,
        in_specs=placed,
        out_specs=(
            P("batch", "seq", None),
            P("batch", "seq", None),
            P("batch", "seq", None),
            P("batch", "seq", None),
            P("seq", None),
        ),
        check_vma=False,
    )
```

```python
import math

import jax
import jax.numpy as jnp
from jax import lax
from jax.experimental import pallas as pl
from jax.experimental.pallas import tpu as pltpu
from jax.sharding import PartitionSpec as P

HEADS = 8
HD = 128
BLK = 128
MEM = 1024
NEAR = 8


def _rows_of(col):
    eye = lax.broadcasted_iota(jnp.int32, (BLK, BLK), 0) == lax.broadcasted_iota(jnp.int32, (BLK, BLK), 1)
    return jnp.sum(jnp.where(eye, col, 0.0), axis=0, keepdims=True)


def _query_body(cnt_ref, nb_ref, q_ref, do_ref, mk_ref, *rest):
    k_refs = rest[:NEAR]
    v_refs = rest[NEAR : 2 * NEAR]
    o_ref, dq_ref, tm_ref, st_ref = rest[2 * NEAR :]
    n = pl.program_id(0)
    h = pl.program_id(1)
    heads = pl.num_programs(1)
    scale = 1.0 / math.sqrt(HD)
    f32 = jnp.float32
    nt = (((1,), (1,)), ((), ()))
    tn = (((0,), (0,)), ((), ()))
    q = q_ref[...]
    do = do_ref[...]
    mk = mk_ref[...]
    nk = jnp.concatenate([r[...] for r in k_refs], axis=0)
    nv = jnp.concatenate([r[...] for r in v_refs], axis=0)
    sm = lax.dot_general(q, mk, nt, preferred_element_type=f32) * scale
    sn = lax.dot_general(q, nk, nt, preferred_element_type=f32) * scale
    col = lax.broadcasted_iota(jnp.int32, sn.shape, 1) // BLK
    sn = jnp.where(col < cnt_ref[n], sn, -jnp.inf)
    m = jnp.maximum(jnp.max(sm, axis=1, keepdims=True), jnp.max(sn, axis=1, keepdims=True))
    em = jnp.exp(sm - m)
    en = jnp.exp(sn - m)
    total = jnp.sum(em, axis=1, keepdims=True) + jnp.sum(en, axis=1, keepdims=True)
    pm = em / total
    pn = en / total
    wm = pm.astype(jnp.bfloat16)
    wn = pn.astype(jnp.bfloat16)
    o = (
        jnp.dot(wm, mk, preferred_element_type=f32) + jnp.dot(wn, nv, preferred_element_type=f32)
    ).astype(jnp.bfloat16)
    o_ref[...] = o
    gd = jnp.sum(do.astype(f32) * o.astype(f32), axis=1, keepdims=True)
    dpm = lax.dot_general(do, mk, nt, preferred_element_type=f32)
    dpn = lax.dot_general(do, nv, nt, preferred_element_type=f32)
    dsm = (pm * (dpm - gd)).astype(jnp.bfloat16)
    dsn = (pn * (dpn - gd)).astype(jnp.bfloat16)
    dq_ref[...] = (
        (jnp.dot(dsm, mk, preferred_element_type=f32) + jnp.dot(dsn, nk, preferred_element_type=f32))
        * scale
    ).astype(jnp.bfloat16)
    tm_ref[0] = lax.dot_general(dsm, q, tn, preferred_element_type=f32) * scale + lax.dot_general(
        wm, do, tn, preferred_element_type=f32
    )
    st_ref[pl.ds(h, 1), :] = _rows_of(m)
    st_ref[pl.ds(heads + h, 1), :] = _rows_of(total)
    st_ref[pl.ds(2 * heads + h, 1), :] = _rows_of(gd)


def query_core(counts, near_rows, q, do, mk, kv_all):
    tokens, width = q.shape
    blocks = tokens // BLK
    mem = mk.shape[0]
    heads = width // HD
    nrows = NEAR * BLK
    qspec = pl.BlockSpec((BLK, HD), lambda n, h, c, t: (n, h))
    mspec = pl.BlockSpec((mem, HD), lambda n, h, c, t: (0, h))

    def kv_spec(j, which):
        return pl.BlockSpec((BLK, HD), lambda n, h, c, t: (t[n * NEAR + j], which * heads + h))

    flops = 2 * tokens * width * (mem + nrows) * 4 + 2 * tokens * width * (nrows + mem * 2)
    grid_spec = pltpu.PrefetchScalarGridSpec(
        num_scalar_prefetch=2,
        grid=(blocks, heads),
        in_specs=[qspec, qspec, mspec]
        + [kv_spec(j, 0) for j in range(NEAR)]
        + [kv_spec(j, 1) for j in range(NEAR)],
        out_specs=[
            qspec,
            qspec,
            pl.BlockSpec((1, mem, HD), lambda n, h, c, t: (n, 0, h)),
            pl.BlockSpec((3 * heads, BLK), lambda n, h, c, t: (0, n)),
        ],
    )
    return pl.pallas_call(
        _query_body,
        grid_spec=grid_spec,
        out_shape=[
            jax.ShapeDtypeStruct((tokens, width), jnp.bfloat16),
            jax.ShapeDtypeStruct((tokens, width), jnp.bfloat16),
            jax.ShapeDtypeStruct((blocks, mem, width), jnp.float32),
            jax.ShapeDtypeStruct((3 * heads, tokens), jnp.float32),
        ],
        compiler_params=pltpu.CompilerParams(dimension_semantics=("arbitrary", "arbitrary")),
        cost_estimate=pl.CostEstimate(
            flops=flops,
            transcendentals=tokens * heads * (mem + nrows),
            bytes_accessed=2 * (4 * tokens * width + blocks * mem * width + 2 * blocks * nrows * width)
            + 4 * blocks * mem * width,
        ),
    )(counts, near_rows, q, do, mk, *([kv_all] * (2 * NEAR)))


def _owner_body(src_blk, src_dev, src_slot, src_live, my_slot, qd_ref, st_ref, k_ref, v_ref, dk_ref, dv_ref):
    s = pl.program_id(0)
    heads = k_ref.shape[1] // HD
    scale = 1.0 / math.sqrt(HD)
    f32 = jnp.float32
    nt = (((1,), (1,)), ((), ()))

    @pl.when(s == 0)
    def _():
        dk_ref[...] = jnp.zeros(dk_ref.shape, f32)
        dv_ref[...] = jnp.zeros(dv_ref.shape, f32)

    @pl.when(src_live[s] != 0)
    def _():
        rows = pl.ds(pl.multiple_of(my_slot[s] * BLK, BLK), BLK)
        st = st_ref[0]
        for h in range(heads):
            cols = pl.ds(h * HD, HD)
            q_h = qd_ref[:, cols]
            do_h = qd_ref[:, pl.ds((heads + h) * HD, HD)]
            k_h = k_ref[rows, cols]
            v_h = v_ref[rows, cols]
            row_max = st[h : h + 1]
            row_total = st[heads + h : heads + h + 1]
            grad_dot = st[2 * heads + h : 2 * heads + h + 1]
            score_t = lax.dot_general(k_h, q_h, nt, preferred_element_type=f32) * scale
            prob_t = jnp.exp(score_t - row_max) / row_total
            weight_t = prob_t.astype(jnp.bfloat16)
            dprob_t = lax.dot_general(v_h, do_h, nt, preferred_element_type=f32)
            dscore_t = (prob_t * (dprob_t - grad_dot)).astype(jnp.bfloat16)
            dk = (jnp.dot(dscore_t, q_h, preferred_element_type=f32) * scale).astype(jnp.bfloat16)
            dv = jnp.dot(weight_t, do_h, preferred_element_type=f32).astype(jnp.bfloat16)
            dk_ref[rows, cols] += dk.astype(f32)
            dv_ref[rows, cols] += dv.astype(f32)


def owner_core(src_blk, src_dev, src_slot, src_live, my_slot, qd_all, stats_all, k_loc, v_loc):
    sources = src_blk.shape[0]
    tokens, width = k_loc.shape
    full = pl.BlockSpec((tokens, width), lambda s, a, e, b, c, d: (0, 0))
    grid_spec = pltpu.PrefetchScalarGridSpec(
        num_scalar_prefetch=5,
        grid=(sources,),
        in_specs=[
            pl.BlockSpec((BLK, 2 * width), lambda s, a, e, b, c, d: (a[s], 0)),
            pl.BlockSpec((1, stats_all.shape[1], BLK), lambda s, a, e, b, c, d: (e[s], 0, b[s])),
            full,
            full,
        ],
        out_specs=[full, full],
    )
    return pl.pallas_call(
        _owner_body,
        grid_spec=grid_spec,
        out_shape=[
            jax.ShapeDtypeStruct((tokens, width), jnp.float32),
            jax.ShapeDtypeStruct((tokens, width), jnp.float32),
        ],
        compiler_params=pltpu.CompilerParams(dimension_semantics=("arbitrary",)),
        cost_estimate=pl.CostEstimate(
            flops=sources * 8 * BLK * BLK * width,
            transcendentals=sources * BLK * BLK * (width // HD),
            bytes_accessed=sources * BLK * 2 * width * 2 + 2 * tokens * width * (2 + 8),
        ),
    )(src_blk, src_dev, src_slot, src_live, my_slot, qd_all, stats_all, k_loc, v_loc)


def shards(
    queries,
    key_states,
    value_states,
    out_grad,
    memory,
    near_device,
    near_slot,
    near_count,
    writer_block,
):
    seq_devices = lax.axis_size("seq")
    batch_devices = lax.axis_size("batch")
    my_index = lax.axis_index("seq")
    tokens = queries.shape[1]
    row_width = queries.shape[2]
    local_blocks = tokens // BLK
    rows_dev = MEM // seq_devices
    block_scale = 1.0 / math.sqrt(BLK)
    value_blocks = value_states[0].reshape(local_blocks, BLK, row_width)

    kv_all = lax.all_gather(
        jnp.concatenate([key_states[0], value_states[0]], axis=-1), "seq", axis=0, tiled=True
    )

    value_sums = jnp.sum(value_blocks, axis=1, dtype=jnp.float32)
    all_sums = lax.all_to_all(
        jnp.broadcast_to(value_sums[None], (seq_devices, local_blocks, row_width)),
        "seq",
        split_axis=0,
        concat_axis=0,
        tiled=True,
    ).reshape(seq_devices * local_blocks, row_width)
    memory_keys = (memory + jnp.take(all_sums, writer_block, axis=0) * block_scale).astype(
        jnp.bfloat16
    )
    near_block = (near_device * local_blocks + near_slot).astype(jnp.int32)
    my_near = lax.dynamic_slice_in_dim(near_block, my_index * local_blocks, local_blocks, 0).reshape(-1)
    my_count = lax.dynamic_slice_in_dim(near_count, my_index * local_blocks, local_blocks, 0)
    qd_all = lax.all_gather(
        jnp.concatenate([queries[0], out_grad[0]], axis=-1), "seq", axis=0, tiled=True
    )
    attended_rows, query_rows_grad, term, stats = query_core(
        my_count, my_near, queries[0], out_grad[0], memory_keys, kv_all
    )
    stats_all = lax.all_to_all(
        jnp.broadcast_to(stats[None], (seq_devices,) + stats.shape),
        "seq",
        split_axis=0,
        concat_axis=0,
        tiled=True,
    )
    row_parts = lax.all_to_all(
        jnp.sum(term, axis=0).astype(jnp.bfloat16).reshape(seq_devices, rows_dev, row_width),
        "seq",
        split_axis=0,
        concat_axis=0,
        tiled=True,
    )
    row_grads = jnp.sum(row_parts.astype(jnp.float32), axis=0)
    near_width = near_device.shape[1]
    entries = local_blocks * near_width
    target = near_device.reshape(seq_devices, entries)
    source_slot = near_slot.reshape(seq_devices, entries)
    live = (
        jnp.arange(near_width)[None, None, :]
        < near_count.reshape(seq_devices, local_blocks)[:, :, None]
    ).reshape(seq_devices, entries)
    names_me = target == my_index
    entry_at = jnp.argmax(names_me, axis=1).astype(jnp.int32)
    src_slot = entry_at // near_width
    src_blk = (jnp.arange(seq_devices, dtype=jnp.int32) * local_blocks + src_slot).astype(jnp.int32)
    src_live = jnp.any(names_me & live, axis=1).astype(jnp.int32)
    my_slot = jnp.sum(jnp.where(names_me, source_slot, 0), axis=1).astype(jnp.int32)
    order = jnp.argsort(1 - src_live, stable=True).astype(jnp.int32)
    live_count = jnp.sum(src_live)
    position = jnp.arange(seq_devices, dtype=jnp.int32)
    pick = jnp.where(position < live_count, order, order[jnp.maximum(live_count - 1, 0)])
    live_in_order = (position < live_count).astype(jnp.int32)
    my_writers = (
        lax.dynamic_slice_in_dim(writer_block, my_index * rows_dev, rows_dev, 0)
        - my_index * local_blocks
    )
    writer_match = (my_writers[:, None] == jnp.arange(local_blocks)[None, :])[:, :, None]
    spread = jnp.sum(jnp.where(writer_match, row_grads[:, None, :], 0.0), axis=0) * block_scale
    all_rows = lax.all_to_all(
        jnp.broadcast_to(row_grads[None], (batch_devices, rows_dev, row_width)),
        "batch",
        split_axis=0,
        concat_axis=0,
        tiled=True,
    )
    memory_grad = jnp.sum(all_rows, axis=0)
    memory_grad, qd_all = lax.optimization_barrier((memory_grad, qd_all))
    dk_sum, dv_sum = owner_core(
        src_blk[pick], pick, src_slot[pick], live_in_order, my_slot[pick], qd_all, stats_all,
        key_states[0], value_states[0],
    )
    value_sum = dv_sum.reshape(local_blocks, BLK, row_width)
    attended = attended_rows.reshape(1, tokens, row_width)
    query_grad = query_rows_grad.reshape(1, tokens, row_width)
    key_grad = dk_sum.astype(jnp.bfloat16).reshape(1, tokens, row_width)
    value_grad = (value_sum + spread[:, None, :]).astype(jnp.bfloat16).reshape(1, tokens, row_width)
    return (attended, query_grad, key_grad, value_grad, memory_grad)


def solution(mesh):
    placed = (
        P("batch", "seq", None),
        P("batch", "seq", None),
        P("batch", "seq", None),
        P("batch", "seq", None),
        P(),
        P(),
        P(),
        P(),
        P(),
    )
    return jax.shard_map(
        shards,
        mesh=mesh,
        in_specs=placed,
        out_specs=(
            P("batch", "seq", None),
            P("batch", "seq", None),
            P("batch", "seq", None),
            P("batch", "seq", None),
            P("seq", None),
        ),
        check_vma=False,
    )
```

```python
import math

import jax
import jax.numpy as jnp
from jax import lax
from jax.experimental import pallas as pl
from jax.experimental.pallas import tpu as pltpu
from jax.sharding import PartitionSpec as P

HEADS = 8
HD = 128
BLK = 128
MEM = 1024
NEAR = 8


def _rows_of(col):
    eye = lax.broadcasted_iota(jnp.int32, (BLK, BLK), 0) == lax.broadcasted_iota(jnp.int32, (BLK, BLK), 1)
    return jnp.sum(jnp.where(eye, col, 0.0), axis=0, keepdims=True)


def _query_body(cnt_ref, nb_ref, q_ref, do_ref, mk_ref, *rest):
    k_refs = rest[:NEAR]
    v_refs = rest[NEAR : 2 * NEAR]
    o_ref, dq_ref, tm_ref, st_ref = rest[2 * NEAR :]
    n = pl.program_id(0)
    h = pl.program_id(1)
    heads = pl.num_programs(1)
    scale = 1.0 / math.sqrt(HD)
    f32 = jnp.float32
    nt = (((1,), (1,)), ((), ()))
    tn = (((0,), (0,)), ((), ()))
    q = q_ref[...]
    do = do_ref[...]
    mk = mk_ref[...]
    nk = jnp.concatenate([r[...] for r in k_refs], axis=0)
    nv = jnp.concatenate([r[...] for r in v_refs], axis=0)
    sm = lax.dot_general(q, mk, nt, preferred_element_type=f32) * scale
    sn = lax.dot_general(q, nk, nt, preferred_element_type=f32) * scale
    col = lax.broadcasted_iota(jnp.int32, sn.shape, 1) // BLK
    sn = jnp.where(col < cnt_ref[n], sn, -jnp.inf)
    m = jnp.maximum(jnp.max(sm, axis=1, keepdims=True), jnp.max(sn, axis=1, keepdims=True))
    em = jnp.exp(sm - m)
    en = jnp.exp(sn - m)
    total = jnp.sum(em, axis=1, keepdims=True) + jnp.sum(en, axis=1, keepdims=True)
    pm = em / total
    pn = en / total
    wm = pm.astype(jnp.bfloat16)
    wn = pn.astype(jnp.bfloat16)
    o = (
        jnp.dot(wm, mk, preferred_element_type=f32) + jnp.dot(wn, nv, preferred_element_type=f32)
    ).astype(jnp.bfloat16)
    o_ref[...] = o
    gd = jnp.sum(do.astype(f32) * o.astype(f32), axis=1, keepdims=True)
    dpm = lax.dot_general(do, mk, nt, preferred_element_type=f32)
    dpn = lax.dot_general(do, nv, nt, preferred_element_type=f32)
    dsm = (pm * (dpm - gd)).astype(jnp.bfloat16)
    dsn = (pn * (dpn - gd)).astype(jnp.bfloat16)
    dq_ref[...] = (
        (jnp.dot(dsm, mk, preferred_element_type=f32) + jnp.dot(dsn, nk, preferred_element_type=f32))
        * scale
    ).astype(jnp.bfloat16)
    tm_ref[0] = lax.dot_general(dsm, q, tn, preferred_element_type=f32) * scale + lax.dot_general(
        wm, do, tn, preferred_element_type=f32
    )
    st_ref[pl.ds(h, 1), :] = _rows_of(m)
    st_ref[pl.ds(heads + h, 1), :] = _rows_of(total)
    st_ref[pl.ds(2 * heads + h, 1), :] = _rows_of(gd)


def query_core(counts, near_rows, q, do, mk, kv_all):
    tokens, width = q.shape
    blocks = tokens // BLK
    mem = mk.shape[0]
    heads = width // HD
    nrows = NEAR * BLK
    qspec = pl.BlockSpec((BLK, HD), lambda n, h, c, t: (n, h))
    mspec = pl.BlockSpec((mem, HD), lambda n, h, c, t: (0, h))

    def kv_spec(j, which):
        return pl.BlockSpec((BLK, HD), lambda n, h, c, t: (t[n * NEAR + j], which * heads + h))

    flops = 2 * tokens * width * (mem + nrows) * 4 + 2 * tokens * width * (nrows + mem * 2)
    grid_spec = pltpu.PrefetchScalarGridSpec(
        num_scalar_prefetch=2,
        grid=(blocks, heads),
        in_specs=[qspec, qspec, mspec]
        + [kv_spec(j, 0) for j in range(NEAR)]
        + [kv_spec(j, 1) for j in range(NEAR)],
        out_specs=[
            qspec,
            qspec,
            pl.BlockSpec((1, mem, HD), lambda n, h, c, t: (n, 0, h)),
            pl.BlockSpec((3 * heads, BLK), lambda n, h, c, t: (0, n)),
        ],
    )
    return pl.pallas_call(
        _query_body,
        grid_spec=grid_spec,
        out_shape=[
            jax.ShapeDtypeStruct((tokens, width), jnp.bfloat16),
            jax.ShapeDtypeStruct((tokens, width), jnp.bfloat16),
            jax.ShapeDtypeStruct((blocks, mem, width), jnp.float32),
            jax.ShapeDtypeStruct((3 * heads, tokens), jnp.float32),
        ],
        compiler_params=pltpu.CompilerParams(dimension_semantics=("arbitrary", "arbitrary")),
        cost_estimate=pl.CostEstimate(
            flops=flops,
            transcendentals=tokens * heads * (mem + nrows),
            bytes_accessed=2 * (4 * tokens * width + blocks * mem * width + 2 * blocks * nrows * width)
            + 4 * blocks * mem * width,
        ),
    )(counts, near_rows, q, do, mk, *([kv_all] * (2 * NEAR)))


def _owner_body(src_blk, src_dev, src_slot, src_live, my_slot, qd_ref, st_ref, k_ref, v_ref, dk_ref, dv_ref):
    s = pl.program_id(0)
    heads = k_ref.shape[1] // HD
    scale = 1.0 / math.sqrt(HD)
    f32 = jnp.float32
    nt = (((1,), (1,)), ((), ()))

    @pl.when(s == 0)
    def _():
        dk_ref[...] = jnp.zeros(dk_ref.shape, f32)
        dv_ref[...] = jnp.zeros(dv_ref.shape, f32)

    @pl.when(src_live[s] != 0)
    def _():
        rows = pl.ds(pl.multiple_of(my_slot[s] * BLK, BLK), BLK)
        st = st_ref[0]
        for h in range(heads):
            cols = pl.ds(h * HD, HD)
            q_h = qd_ref[:, cols]
            do_h = qd_ref[:, pl.ds((heads + h) * HD, HD)]
            k_h = k_ref[rows, cols]
            v_h = v_ref[rows, cols]
            row_max = st[h : h + 1]
            row_total = st[heads + h : heads + h + 1]
            grad_dot = st[2 * heads + h : 2 * heads + h + 1]
            score_t = lax.dot_general(k_h, q_h, nt, preferred_element_type=f32) * scale
            prob_t = jnp.exp(score_t - row_max) / row_total
            weight_t = prob_t.astype(jnp.bfloat16)
            dprob_t = lax.dot_general(v_h, do_h, nt, preferred_element_type=f32)
            dscore_t = (prob_t * (dprob_t - grad_dot)).astype(jnp.bfloat16)
            dk = (jnp.dot(dscore_t, q_h, preferred_element_type=f32) * scale).astype(jnp.bfloat16)
            dv = jnp.dot(weight_t, do_h, preferred_element_type=f32).astype(jnp.bfloat16)
            dk_ref[rows, cols] += dk.astype(f32)
            dv_ref[rows, cols] += dv.astype(f32)


def owner_core(src_blk, src_dev, src_slot, src_live, my_slot, qd_all, stats_all, k_loc, v_loc):
    sources = src_blk.shape[0]
    tokens, width = k_loc.shape
    full = pl.BlockSpec((tokens, width), lambda s, a, e, b, c, d: (0, 0))
    grid_spec = pltpu.PrefetchScalarGridSpec(
        num_scalar_prefetch=5,
        grid=(sources,),
        in_specs=[
            pl.BlockSpec((BLK, 2 * width), lambda s, a, e, b, c, d: (a[s], 0)),
            pl.BlockSpec((1, stats_all.shape[1], BLK), lambda s, a, e, b, c, d: (e[s], 0, b[s])),
            full,
            full,
        ],
        out_specs=[full, full],
    )
    return pl.pallas_call(
        _owner_body,
        grid_spec=grid_spec,
        out_shape=[
            jax.ShapeDtypeStruct((tokens, width), jnp.float32),
            jax.ShapeDtypeStruct((tokens, width), jnp.float32),
        ],
        compiler_params=pltpu.CompilerParams(dimension_semantics=("arbitrary",)),
        cost_estimate=pl.CostEstimate(
            flops=sources * 8 * BLK * BLK * width,
            transcendentals=sources * BLK * BLK * (width // HD),
            bytes_accessed=sources * BLK * 2 * width * 2 + 2 * tokens * width * (2 + 8),
        ),
    )(src_blk, src_dev, src_slot, src_live, my_slot, qd_all, stats_all, k_loc, v_loc)


def shards(
    queries,
    key_states,
    value_states,
    out_grad,
    memory,
    near_device,
    near_slot,
    near_count,
    writer_block,
):
    seq_devices = lax.axis_size("seq")
    batch_devices = lax.axis_size("batch")
    my_index = lax.axis_index("seq")
    tokens = queries.shape[1]
    row_width = queries.shape[2]
    local_blocks = tokens // BLK
    rows_dev = MEM // seq_devices
    block_scale = 1.0 / math.sqrt(BLK)
    value_blocks = value_states[0].reshape(local_blocks, BLK, row_width)

    kv_all = lax.all_gather(
        jnp.concatenate([key_states[0], value_states[0]], axis=-1), "seq", axis=0, tiled=True
    )

    value_sums = jnp.sum(value_blocks, axis=1, dtype=jnp.float32)
    all_sums = lax.all_to_all(
        jnp.broadcast_to(value_sums[None], (seq_devices, local_blocks, row_width)),
        "seq",
        split_axis=0,
        concat_axis=0,
        tiled=True,
    ).reshape(seq_devices * local_blocks, row_width)
    memory_keys = (memory + jnp.take(all_sums, writer_block, axis=0) * block_scale).astype(
        jnp.bfloat16
    )
    near_block = (near_device * local_blocks + near_slot).astype(jnp.int32)
    my_near = lax.dynamic_slice_in_dim(near_block, my_index * local_blocks, local_blocks, 0).reshape(-1)
    my_count = lax.dynamic_slice_in_dim(near_count, my_index * local_blocks, local_blocks, 0)
    qd_all = lax.all_gather(
        jnp.concatenate([queries[0], out_grad[0]], axis=-1), "seq", axis=0, tiled=True
    )
    attended_rows, query_rows_grad, term, stats = query_core(
        my_count, my_near, queries[0], out_grad[0], memory_keys, kv_all
    )
    stats_all = lax.all_to_all(
        jnp.broadcast_to(stats[None], (seq_devices,) + stats.shape),
        "seq",
        split_axis=0,
        concat_axis=0,
        tiled=True,
    )
    term_rows, qd_all = lax.optimization_barrier((jnp.sum(term, axis=0).astype(jnp.bfloat16), qd_all))
    row_parts = lax.all_to_all(
        term_rows.reshape(seq_devices, rows_dev, row_width),
        "seq",
        split_axis=0,
        concat_axis=0,
        tiled=True,
    )
    row_grads = jnp.sum(row_parts.astype(jnp.float32), axis=0)
    near_width = near_device.shape[1]
    entries = local_blocks * near_width
    target = near_device.reshape(seq_devices, entries)
    source_slot = near_slot.reshape(seq_devices, entries)
    live = (
        jnp.arange(near_width)[None, None, :]
        < near_count.reshape(seq_devices, local_blocks)[:, :, None]
    ).reshape(seq_devices, entries)
    names_me = target == my_index
    entry_at = jnp.argmax(names_me, axis=1).astype(jnp.int32)
    src_slot = entry_at // near_width
    src_blk = (jnp.arange(seq_devices, dtype=jnp.int32) * local_blocks + src_slot).astype(jnp.int32)
    src_live = jnp.any(names_me & live, axis=1).astype(jnp.int32)
    my_slot = jnp.sum(jnp.where(names_me, source_slot, 0), axis=1).astype(jnp.int32)
    order = jnp.argsort(1 - src_live, stable=True).astype(jnp.int32)
    live_count = jnp.sum(src_live)
    position = jnp.arange(seq_devices, dtype=jnp.int32)
    pick = jnp.where(position < live_count, order, order[jnp.maximum(live_count - 1, 0)])
    live_in_order = (position < live_count).astype(jnp.int32)
    my_writers = (
        lax.dynamic_slice_in_dim(writer_block, my_index * rows_dev, rows_dev, 0)
        - my_index * local_blocks
    )
    writer_match = (my_writers[:, None] == jnp.arange(local_blocks)[None, :])[:, :, None]
    spread = jnp.sum(jnp.where(writer_match, row_grads[:, None, :], 0.0), axis=0) * block_scale
    all_rows = lax.all_to_all(
        jnp.broadcast_to(row_grads[None], (batch_devices, rows_dev, row_width)),
        "batch",
        split_axis=0,
        concat_axis=0,
        tiled=True,
    )
    memory_grad = jnp.sum(all_rows, axis=0)
    dk_sum, dv_sum = owner_core(
        src_blk[pick], pick, src_slot[pick], live_in_order, my_slot[pick], qd_all, stats_all,
        key_states[0], value_states[0],
    )
    value_sum = dv_sum.reshape(local_blocks, BLK, row_width)
    attended = attended_rows.reshape(1, tokens, row_width)
    query_grad = query_rows_grad.reshape(1, tokens, row_width)
    key_grad = dk_sum.astype(jnp.bfloat16).reshape(1, tokens, row_width)
    value_grad = (value_sum + spread[:, None, :]).astype(jnp.bfloat16).reshape(1, tokens, row_width)
    return (attended, query_grad, key_grad, value_grad, memory_grad)


def solution(mesh):
    placed = (
        P("batch", "seq", None),
        P("batch", "seq", None),
        P("batch", "seq", None),
        P("batch", "seq", None),
        P(),
        P(),
        P(),
        P(),
        P(),
    )
    return jax.shard_map(
        shards,
        mesh=mesh,
        in_specs=placed,
        out_specs=(
            P("batch", "seq", None),
            P("batch", "seq", None),
            P("batch", "seq", None),
            P("batch", "seq", None),
            P("seq", None),
        ),
        check_vma=False,
    )
```

```python
import math

import jax
import jax.numpy as jnp
from jax import lax
from jax.experimental import pallas as pl
from jax.experimental.pallas import tpu as pltpu
from jax.sharding import PartitionSpec as P

HEADS = 8
HD = 128
BLK = 128
MEM = 1024
NEAR = 8


def _rows_of(col):
    eye = lax.broadcasted_iota(jnp.int32, (BLK, BLK), 0) == lax.broadcasted_iota(jnp.int32, (BLK, BLK), 1)
    return jnp.sum(jnp.where(eye, col, 0.0), axis=0, keepdims=True)


def _query_body(cnt_ref, nb_ref, q_ref, do_ref, mk_ref, *rest):
    k_refs = rest[:NEAR]
    v_refs = rest[NEAR : 2 * NEAR]
    o_ref, dq_ref, tm_ref, st_ref = rest[2 * NEAR :]
    n = pl.program_id(0)
    h = pl.program_id(1)
    heads = pl.num_programs(1)
    scale = 1.0 / math.sqrt(HD)
    f32 = jnp.float32
    nt = (((1,), (1,)), ((), ()))
    tn = (((0,), (0,)), ((), ()))
    q = q_ref[...]
    do = do_ref[...]
    mk = mk_ref[...]
    nk = jnp.concatenate([r[...] for r in k_refs], axis=0)
    nv = jnp.concatenate([r[...] for r in v_refs], axis=0)
    sm = lax.dot_general(q, mk, nt, preferred_element_type=f32) * scale
    sn = lax.dot_general(q, nk, nt, preferred_element_type=f32) * scale
    col = lax.broadcasted_iota(jnp.int32, sn.shape, 1) // BLK
    sn = jnp.where(col < cnt_ref[n], sn, -jnp.inf)
    m = jnp.maximum(jnp.max(sm, axis=1, keepdims=True), jnp.max(sn, axis=1, keepdims=True))
    em = jnp.exp(sm - m)
    en = jnp.exp(sn - m)
    total = jnp.sum(em, axis=1, keepdims=True) + jnp.sum(en, axis=1, keepdims=True)
    pm = em / total
    pn = en / total
    wm = pm.astype(jnp.bfloat16)
    wn = pn.astype(jnp.bfloat16)
    o = (
        jnp.dot(wm, mk, preferred_element_type=f32) + jnp.dot(wn, nv, preferred_element_type=f32)
    ).astype(jnp.bfloat16)
    o_ref[...] = o
    gd = jnp.sum(do.astype(f32) * o.astype(f32), axis=1, keepdims=True)
    dpm = lax.dot_general(do, mk, nt, preferred_element_type=f32)
    dpn = lax.dot_general(do, nv, nt, preferred_element_type=f32)
    dsm = (pm * (dpm - gd)).astype(jnp.bfloat16)
    dsn = (pn * (dpn - gd)).astype(jnp.bfloat16)
    dq_ref[...] = (
        (jnp.dot(dsm, mk, preferred_element_type=f32) + jnp.dot(dsn, nk, preferred_element_type=f32))
        * scale
    ).astype(jnp.bfloat16)
    tm_ref[0] = lax.dot_general(dsm, q, tn, preferred_element_type=f32) * scale + lax.dot_general(
        wm, do, tn, preferred_element_type=f32
    )
    st_ref[pl.ds(h, 1), :] = _rows_of(m)
    st_ref[pl.ds(heads + h, 1), :] = _rows_of(total)
    st_ref[pl.ds(2 * heads + h, 1), :] = _rows_of(gd)


def query_core(counts, near_rows, q, do, mk, kv_all):
    tokens, width = q.shape
    blocks = tokens // BLK
    mem = mk.shape[0]
    heads = width // HD
    nrows = NEAR * BLK
    qspec = pl.BlockSpec((BLK, HD), lambda n, h, c, t: (n, h))
    mspec = pl.BlockSpec((mem, HD), lambda n, h, c, t: (0, h))

    def kv_spec(j, which):
        return pl.BlockSpec((BLK, HD), lambda n, h, c, t: (t[n * NEAR + j], which * heads + h))

    flops = 2 * tokens * width * (mem + nrows) * 4 + 2 * tokens * width * (nrows + mem * 2)
    grid_spec = pltpu.PrefetchScalarGridSpec(
        num_scalar_prefetch=2,
        grid=(blocks, heads),
        in_specs=[qspec, qspec, mspec]
        + [kv_spec(j, 0) for j in range(NEAR)]
        + [kv_spec(j, 1) for j in range(NEAR)],
        out_specs=[
            qspec,
            qspec,
            pl.BlockSpec((1, mem, HD), lambda n, h, c, t: (n, 0, h)),
            pl.BlockSpec((3 * heads, BLK), lambda n, h, c, t: (0, n)),
        ],
    )
    return pl.pallas_call(
        _query_body,
        grid_spec=grid_spec,
        out_shape=[
            jax.ShapeDtypeStruct((tokens, width), jnp.bfloat16),
            jax.ShapeDtypeStruct((tokens, width), jnp.bfloat16),
            jax.ShapeDtypeStruct((blocks, mem, width), jnp.float32),
            jax.ShapeDtypeStruct((3 * heads, tokens), jnp.float32),
        ],
        compiler_params=pltpu.CompilerParams(dimension_semantics=("arbitrary", "arbitrary")),
        cost_estimate=pl.CostEstimate(
            flops=flops,
            transcendentals=tokens * heads * (mem + nrows),
            bytes_accessed=2 * (4 * tokens * width + blocks * mem * width + 2 * blocks * nrows * width)
            + 4 * blocks * mem * width,
        ),
    )(counts, near_rows, q, do, mk, *([kv_all] * (2 * NEAR)))


def _owner_body(
    src_blk, src_dev, src_slot, src_live, my_slot, qd_ref, st_ref, k_ref, v_ref, sp_ref, dk_out, dv_out, dk_ref, dv_ref
):
    s = pl.program_id(0)
    heads = k_ref.shape[1] // HD
    scale = 1.0 / math.sqrt(HD)
    f32 = jnp.float32
    nt = (((1,), (1,)), ((), ()))

    @pl.when(s == 0)
    def _():
        dk_ref[...] = jnp.zeros(dk_ref.shape, f32)
        dv_ref[...] = jnp.zeros(dv_ref.shape, f32)

    @pl.when(src_live[s] != 0)
    def _():
        rows = pl.ds(pl.multiple_of(my_slot[s] * BLK, BLK), BLK)
        st = st_ref[0]
        for h in range(heads):
            cols = pl.ds(h * HD, HD)
            q_h = qd_ref[:, cols]
            do_h = qd_ref[:, pl.ds((heads + h) * HD, HD)]
            k_h = k_ref[rows, cols]
            v_h = v_ref[rows, cols]
            row_max = st[h : h + 1]
            row_total = st[heads + h : heads + h + 1]
            grad_dot = st[2 * heads + h : 2 * heads + h + 1]
            score_t = lax.dot_general(k_h, q_h, nt, preferred_element_type=f32) * scale
            prob_t = jnp.exp(score_t - row_max) / row_total
            weight_t = prob_t.astype(jnp.bfloat16)
            dprob_t = lax.dot_general(v_h, do_h, nt, preferred_element_type=f32)
            dscore_t = (prob_t * (dprob_t - grad_dot)).astype(jnp.bfloat16)
            dk = (jnp.dot(dscore_t, q_h, preferred_element_type=f32) * scale).astype(jnp.bfloat16)
            dv = jnp.dot(weight_t, do_h, preferred_element_type=f32).astype(jnp.bfloat16)
            dk_ref[rows, cols] += dk.astype(f32)
            dv_ref[rows, cols] += dv.astype(f32)

    @pl.when(s == pl.num_programs(0) - 1)
    def _():
        dk_out[...] = dk_ref[...].astype(dk_out.dtype)
        for l in range(dk_ref.shape[0] // BLK):
            block_rows = slice(l * BLK, (l + 1) * BLK)
            dv_out[block_rows, :] = (dv_ref[block_rows, :] + sp_ref[l : l + 1, :]).astype(dv_out.dtype)


def owner_core(src_blk, src_dev, src_slot, src_live, my_slot, qd_all, stats_all, k_loc, v_loc, spread):
    sources = src_blk.shape[0]
    tokens, width = k_loc.shape
    full = pl.BlockSpec((tokens, width), lambda s, a, e, b, c, d: (0, 0))
    grid_spec = pltpu.PrefetchScalarGridSpec(
        num_scalar_prefetch=5,
        grid=(sources,),
        in_specs=[
            pl.BlockSpec((BLK, 2 * width), lambda s, a, e, b, c, d: (a[s], 0)),
            pl.BlockSpec((1, stats_all.shape[1], BLK), lambda s, a, e, b, c, d: (e[s], 0, b[s])),
            full,
            full,
            pl.BlockSpec(spread.shape, lambda s, a, e, b, c, d: (0, 0)),
        ],
        out_specs=[full, full],
        scratch_shapes=[pltpu.VMEM((tokens, width), jnp.float32), pltpu.VMEM((tokens, width), jnp.float32)],
    )
    return pl.pallas_call(
        _owner_body,
        grid_spec=grid_spec,
        out_shape=[
            jax.ShapeDtypeStruct((tokens, width), jnp.bfloat16),
            jax.ShapeDtypeStruct((tokens, width), jnp.bfloat16),
        ],
        compiler_params=pltpu.CompilerParams(dimension_semantics=("arbitrary",)),
        cost_estimate=pl.CostEstimate(
            flops=sources * 8 * BLK * BLK * width,
            transcendentals=sources * BLK * BLK * (width // HD),
            bytes_accessed=sources * BLK * 2 * width * 2 + 2 * tokens * width * (2 + 8),
        ),
    )(src_blk, src_dev, src_slot, src_live, my_slot, qd_all, stats_all, k_loc, v_loc, spread)


def shards(
    queries,
    key_states,
    value_states,
    out_grad,
    memory,
    near_device,
    near_slot,
    near_count,
    writer_block,
):
    seq_devices = lax.axis_size("seq")
    batch_devices = lax.axis_size("batch")
    my_index = lax.axis_index("seq")
    tokens = queries.shape[1]
    row_width = queries.shape[2]
    local_blocks = tokens // BLK
    rows_dev = MEM // seq_devices
    block_scale = 1.0 / math.sqrt(BLK)
    value_blocks = value_states[0].reshape(local_blocks, BLK, row_width)

    kv_all = lax.all_gather(
        jnp.concatenate([key_states[0], value_states[0]], axis=-1), "seq", axis=0, tiled=True
    )

    value_sums = jnp.sum(value_blocks, axis=1, dtype=jnp.float32)
    all_sums = lax.all_to_all(
        jnp.broadcast_to(value_sums[None], (seq_devices, local_blocks, row_width)),
        "seq",
        split_axis=0,
        concat_axis=0,
        tiled=True,
    ).reshape(seq_devices * local_blocks, row_width)
    memory_keys = (memory + jnp.take(all_sums, writer_block, axis=0) * block_scale).astype(
        jnp.bfloat16
    )
    near_block = (near_device * local_blocks + near_slot).astype(jnp.int32)
    my_near = lax.dynamic_slice_in_dim(near_block, my_index * local_blocks, local_blocks, 0).reshape(-1)
    my_count = lax.dynamic_slice_in_dim(near_count, my_index * local_blocks, local_blocks, 0)
    qd_all = lax.all_gather(
        jnp.concatenate([queries[0], out_grad[0]], axis=-1), "seq", axis=0, tiled=True
    )
    attended_rows, query_rows_grad, term, stats = query_core(
        my_count, my_near, queries[0], out_grad[0], memory_keys, kv_all
    )
    stats_all = lax.all_to_all(
        jnp.broadcast_to(stats[None], (seq_devices,) + stats.shape),
        "seq",
        split_axis=0,
        concat_axis=0,
        tiled=True,
    )
    row_parts = lax.all_to_all(
        jnp.sum(term, axis=0).astype(jnp.bfloat16).reshape(seq_devices, rows_dev, row_width),
        "seq",
        split_axis=0,
        concat_axis=0,
        tiled=True,
    )
    row_grads = jnp.sum(row_parts.astype(jnp.float32), axis=0)
    near_width = near_device.shape[1]
    entries = local_blocks * near_width
    target = near_device.reshape(seq_devices, entries)
    source_slot = near_slot.reshape(seq_devices, entries)
    live = (
        jnp.arange(near_width)[None, None, :]
        < near_count.reshape(seq_devices, local_blocks)[:, :, None]
    ).reshape(seq_devices, entries)
    names_me = target == my_index
    entry_at = jnp.argmax(names_me, axis=1).astype(jnp.int32)
    src_slot = entry_at // near_width
    src_blk = (jnp.arange(seq_devices, dtype=jnp.int32) * local_blocks + src_slot).astype(jnp.int32)
    src_live = jnp.any(names_me & live, axis=1).astype(jnp.int32)
    my_slot = jnp.sum(jnp.where(names_me, source_slot, 0), axis=1).astype(jnp.int32)
    order = jnp.argsort(1 - src_live, stable=True).astype(jnp.int32)
    live_count = jnp.sum(src_live)
    position = jnp.arange(seq_devices, dtype=jnp.int32)
    pick = jnp.where(position < live_count, order, order[jnp.maximum(live_count - 1, 0)])
    live_in_order = (position < live_count).astype(jnp.int32)
    my_writers = (
        lax.dynamic_slice_in_dim(writer_block, my_index * rows_dev, rows_dev, 0)
        - my_index * local_blocks
    )
    writer_match = (my_writers[:, None] == jnp.arange(local_blocks)[None, :])[:, :, None]
    spread = jnp.sum(jnp.where(writer_match, row_grads[:, None, :], 0.0), axis=0) * block_scale
    all_rows = lax.all_to_all(
        jnp.broadcast_to(row_grads[None], (batch_devices, rows_dev, row_width)),
        "batch",
        split_axis=0,
        concat_axis=0,
        tiled=True,
    )
    memory_grad = jnp.sum(all_rows, axis=0)
    memory_grad, qd_all = lax.optimization_barrier((memory_grad, qd_all))
    dk_sum, dv_sum = owner_core(
        src_blk[pick], pick, src_slot[pick], live_in_order, my_slot[pick], qd_all, stats_all,
        key_states[0], value_states[0], spread,
    )
    attended = attended_rows.reshape(1, tokens, row_width)
    query_grad = query_rows_grad.reshape(1, tokens, row_width)
    key_grad = dk_sum.reshape(1, tokens, row_width)
    value_grad = dv_sum.reshape(1, tokens, row_width)
    return (attended, query_grad, key_grad, value_grad, memory_grad)


def solution(mesh):
    placed = (
        P("batch", "seq", None),
        P("batch", "seq", None),
        P("batch", "seq", None),
        P("batch", "seq", None),
        P(),
        P(),
        P(),
        P(),
        P(),
    )
    return jax.shard_map(
        shards,
        mesh=mesh,
        in_specs=placed,
        out_specs=(
            P("batch", "seq", None),
            P("batch", "seq", None),
            P("batch", "seq", None),
            P("batch", "seq", None),
            P("seq", None),
        ),
        check_vma=False,
    )
```

```python
import math

import jax
import jax.numpy as jnp
from jax import lax
from jax.experimental import pallas as pl
from jax.experimental.pallas import tpu as pltpu
from jax.sharding import PartitionSpec as P

HEADS = 8
HD = 128
BLK = 128
MEM = 1024
NEAR = 8


def _rows_of(col):
    eye = lax.broadcasted_iota(jnp.int32, (BLK, BLK), 0) == lax.broadcasted_iota(jnp.int32, (BLK, BLK), 1)
    return jnp.sum(jnp.where(eye, col, 0.0), axis=0, keepdims=True)


def _query_body(cnt_ref, nb_ref, q_ref, do_ref, mk_ref, *rest):
    k_refs = rest[:NEAR]
    v_refs = rest[NEAR : 2 * NEAR]
    o_ref, dq_ref, tm_ref, st_ref = rest[2 * NEAR :]
    n = pl.program_id(0)
    h = pl.program_id(1)
    heads = pl.num_programs(1)
    scale = 1.0 / math.sqrt(HD)
    f32 = jnp.float32
    nt = (((1,), (1,)), ((), ()))
    tn = (((0,), (0,)), ((), ()))
    q = q_ref[...]
    do = do_ref[...]
    mk = mk_ref[...]
    nk = jnp.concatenate([r[...] for r in k_refs], axis=0)
    nv = jnp.concatenate([r[...] for r in v_refs], axis=0)
    sm = lax.dot_general(q, mk, nt, preferred_element_type=f32) * scale
    sn = lax.dot_general(q, nk, nt, preferred_element_type=f32) * scale
    col = lax.broadcasted_iota(jnp.int32, sn.shape, 1) // BLK
    sn = jnp.where(col < cnt_ref[n], sn, -jnp.inf)
    m = jnp.maximum(jnp.max(sm, axis=1, keepdims=True), jnp.max(sn, axis=1, keepdims=True))
    em = jnp.exp(sm - m)
    en = jnp.exp(sn - m)
    total = jnp.sum(em, axis=1, keepdims=True) + jnp.sum(en, axis=1, keepdims=True)
    pm = em / total
    pn = en / total
    wm = pm.astype(jnp.bfloat16)
    wn = pn.astype(jnp.bfloat16)
    o = (
        jnp.dot(wm, mk, preferred_element_type=f32) + jnp.dot(wn, nv, preferred_element_type=f32)
    ).astype(jnp.bfloat16)
    o_ref[...] = o
    gd = jnp.sum(do.astype(f32) * o.astype(f32), axis=1, keepdims=True)
    dpm = lax.dot_general(do, mk, nt, preferred_element_type=f32)
    dpn = lax.dot_general(do, nv, nt, preferred_element_type=f32)
    dsm = (pm * (dpm - gd)).astype(jnp.bfloat16)
    dsn = (pn * (dpn - gd)).astype(jnp.bfloat16)
    dq_ref[...] = (
        (jnp.dot(dsm, mk, preferred_element_type=f32) + jnp.dot(dsn, nk, preferred_element_type=f32))
        * scale
    ).astype(jnp.bfloat16)
    tm_ref[0] = lax.dot_general(dsm, q, tn, preferred_element_type=f32) * scale + lax.dot_general(
        wm, do, tn, preferred_element_type=f32
    )
    st_ref[pl.ds(h, 1), :] = _rows_of(m)
    st_ref[pl.ds(heads + h, 1), :] = _rows_of(total)
    st_ref[pl.ds(2 * heads + h, 1), :] = _rows_of(gd)


def query_core(counts, near_rows, q, do, mk, kv_all):
    tokens, width = q.shape
    blocks = tokens // BLK
    mem = mk.shape[0]
    heads = width // HD
    nrows = NEAR * BLK
    qspec = pl.BlockSpec((BLK, HD), lambda n, h, c, t: (n, h))
    mspec = pl.BlockSpec((mem, HD), lambda n, h, c, t: (0, h))

    def kv_spec(j, which):
        return pl.BlockSpec((BLK, HD), lambda n, h, c, t: (t[n * NEAR + j], which * heads + h))

    flops = 2 * tokens * width * (mem + nrows) * 4 + 2 * tokens * width * (nrows + mem * 2)
    grid_spec = pltpu.PrefetchScalarGridSpec(
        num_scalar_prefetch=2,
        grid=(blocks, heads),
        in_specs=[qspec, qspec, mspec]
        + [kv_spec(j, 0) for j in range(NEAR)]
        + [kv_spec(j, 1) for j in range(NEAR)],
        out_specs=[
            qspec,
            qspec,
            pl.BlockSpec((1, mem, HD), lambda n, h, c, t: (n, 0, h)),
            pl.BlockSpec((3 * heads, BLK), lambda n, h, c, t: (0, n)),
        ],
    )
    return pl.pallas_call(
        _query_body,
        grid_spec=grid_spec,
        out_shape=[
            jax.ShapeDtypeStruct((tokens, width), jnp.bfloat16),
            jax.ShapeDtypeStruct((tokens, width), jnp.bfloat16),
            jax.ShapeDtypeStruct((blocks, mem, width), jnp.float32),
            jax.ShapeDtypeStruct((3 * heads, tokens), jnp.float32),
        ],
        compiler_params=pltpu.CompilerParams(dimension_semantics=("arbitrary", "arbitrary")),
        cost_estimate=pl.CostEstimate(
            flops=flops,
            transcendentals=tokens * heads * (mem + nrows),
            bytes_accessed=2 * (4 * tokens * width + blocks * mem * width + 2 * blocks * nrows * width)
            + 4 * blocks * mem * width,
        ),
    )(counts, near_rows, q, do, mk, *([kv_all] * (2 * NEAR)))


def _owner_body(
    src_blk, src_dev, src_slot, src_live, my_slot, qd_ref, st_ref, k_ref, v_ref, sp_ref, dk_out, dv_out, dk_ref, dv_ref
):
    s = pl.program_id(0)
    heads = k_ref.shape[1] // HD
    scale = 1.0 / math.sqrt(HD)
    f32 = jnp.float32
    nt = (((1,), (1,)), ((), ()))

    @pl.when(s == 0)
    def _():
        dk_ref[...] = jnp.zeros(dk_ref.shape, f32)
        dv_ref[...] = jnp.zeros(dv_ref.shape, f32)

    @pl.when(src_live[s] != 0)
    def _():
        rows = pl.ds(pl.multiple_of(my_slot[s] * BLK, BLK), BLK)
        st = st_ref[0]
        for h in range(heads):
            cols = pl.ds(h * HD, HD)
            q_h = qd_ref[:, cols]
            do_h = qd_ref[:, pl.ds((heads + h) * HD, HD)]
            k_h = k_ref[rows, cols]
            v_h = v_ref[rows, cols]
            row_max = st[h : h + 1]
            row_total = st[heads + h : heads + h + 1]
            grad_dot = st[2 * heads + h : 2 * heads + h + 1]
            score_t = lax.dot_general(k_h, q_h, nt, preferred_element_type=f32) * scale
            prob_t = jnp.exp(score_t - row_max) * (1.0 / row_total)
            weight_t = prob_t.astype(jnp.bfloat16)
            dprob_t = lax.dot_general(v_h, do_h, nt, preferred_element_type=f32)
            dscore_t = (prob_t * (dprob_t - grad_dot)).astype(jnp.bfloat16)
            dk = (jnp.dot(dscore_t, q_h, preferred_element_type=f32) * scale).astype(jnp.bfloat16)
            dv = jnp.dot(weight_t, do_h, preferred_element_type=f32).astype(jnp.bfloat16)
            dk_ref[rows, cols] += dk.astype(f32)
            dv_ref[rows, cols] += dv.astype(f32)

    @pl.when(s == pl.num_programs(0) - 1)
    def _():
        dk_out[...] = dk_ref[...].astype(dk_out.dtype)
        for l in range(dk_ref.shape[0] // BLK):
            block_rows = slice(l * BLK, (l + 1) * BLK)
            dv_out[block_rows, :] = (dv_ref[block_rows, :] + sp_ref[l : l + 1, :]).astype(dv_out.dtype)


def owner_core(src_blk, src_dev, src_slot, src_live, my_slot, qd_all, stats_all, k_loc, v_loc, spread):
    sources = src_blk.shape[0]
    tokens, width = k_loc.shape
    full = pl.BlockSpec((tokens, width), lambda s, a, e, b, c, d: (0, 0))
    grid_spec = pltpu.PrefetchScalarGridSpec(
        num_scalar_prefetch=5,
        grid=(sources,),
        in_specs=[
            pl.BlockSpec((BLK, 2 * width), lambda s, a, e, b, c, d: (a[s], 0)),
            pl.BlockSpec((1, stats_all.shape[1], BLK), lambda s, a, e, b, c, d: (e[s], 0, b[s])),
            full,
            full,
            pl.BlockSpec(spread.shape, lambda s, a, e, b, c, d: (0, 0)),
        ],
        out_specs=[full, full],
        scratch_shapes=[pltpu.VMEM((tokens, width), jnp.float32), pltpu.VMEM((tokens, width), jnp.float32)],
    )
    return pl.pallas_call(
        _owner_body,
        grid_spec=grid_spec,
        out_shape=[
            jax.ShapeDtypeStruct((tokens, width), jnp.bfloat16),
            jax.ShapeDtypeStruct((tokens, width), jnp.bfloat16),
        ],
        compiler_params=pltpu.CompilerParams(dimension_semantics=("arbitrary",)),
        cost_estimate=pl.CostEstimate(
            flops=sources * 8 * BLK * BLK * width,
            transcendentals=sources * BLK * BLK * (width // HD),
            bytes_accessed=sources * BLK * 2 * width * 2 + 2 * tokens * width * (2 + 8),
        ),
    )(src_blk, src_dev, src_slot, src_live, my_slot, qd_all, stats_all, k_loc, v_loc, spread)


def shards(
    queries,
    key_states,
    value_states,
    out_grad,
    memory,
    near_device,
    near_slot,
    near_count,
    writer_block,
):
    seq_devices = lax.axis_size("seq")
    batch_devices = lax.axis_size("batch")
    my_index = lax.axis_index("seq")
    tokens = queries.shape[1]
    row_width = queries.shape[2]
    local_blocks = tokens // BLK
    rows_dev = MEM // seq_devices
    block_scale = 1.0 / math.sqrt(BLK)
    value_blocks = value_states[0].reshape(local_blocks, BLK, row_width)

    kv_all = lax.all_gather(
        jnp.concatenate([key_states[0], value_states[0]], axis=-1), "seq", axis=0, tiled=True
    )

    value_sums = jnp.sum(value_blocks, axis=1, dtype=jnp.float32)
    all_sums = lax.all_to_all(
        jnp.broadcast_to(value_sums[None], (seq_devices, local_blocks, row_width)),
        "seq",
        split_axis=0,
        concat_axis=0,
        tiled=True,
    ).reshape(seq_devices * local_blocks, row_width)
    memory_keys = (memory + jnp.take(all_sums, writer_block, axis=0) * block_scale).astype(
        jnp.bfloat16
    )
    near_block = (near_device * local_blocks + near_slot).astype(jnp.int32)
    my_near = lax.dynamic_slice_in_dim(near_block, my_index * local_blocks, local_blocks, 0).reshape(-1)
    my_count = lax.dynamic_slice_in_dim(near_count, my_index * local_blocks, local_blocks, 0)
    qd_all = lax.all_gather(
        jnp.concatenate([queries[0], out_grad[0]], axis=-1), "seq", axis=0, tiled=True
    )
    attended_rows, query_rows_grad, term, stats = query_core(
        my_count, my_near, queries[0], out_grad[0], memory_keys, kv_all
    )
    stats_all = lax.all_to_all(
        jnp.broadcast_to(stats[None], (seq_devices,) + stats.shape),
        "seq",
        split_axis=0,
        concat_axis=0,
        tiled=True,
    )
    row_parts = lax.all_to_all(
        jnp.sum(term, axis=0).astype(jnp.bfloat16).reshape(seq_devices, rows_dev, row_width),
        "seq",
        split_axis=0,
        concat_axis=0,
        tiled=True,
    )
    row_grads = jnp.sum(row_parts.astype(jnp.float32), axis=0)
    near_width = near_device.shape[1]
    entries = local_blocks * near_width
    target = near_device.reshape(seq_devices, entries)
    source_slot = near_slot.reshape(seq_devices, entries)
    live = (
        jnp.arange(near_width)[None, None, :]
        < near_count.reshape(seq_devices, local_blocks)[:, :, None]
    ).reshape(seq_devices, entries)
    names_me = target == my_index
    entry_at = jnp.argmax(names_me, axis=1).astype(jnp.int32)
    src_slot = entry_at // near_width
    src_blk = (jnp.arange(seq_devices, dtype=jnp.int32) * local_blocks + src_slot).astype(jnp.int32)
    src_live = jnp.any(names_me & live, axis=1).astype(jnp.int32)
    my_slot = jnp.sum(jnp.where(names_me, source_slot, 0), axis=1).astype(jnp.int32)
    order = jnp.argsort(1 - src_live, stable=True).astype(jnp.int32)
    live_count = jnp.sum(src_live)
    position = jnp.arange(seq_devices, dtype=jnp.int32)
    pick = jnp.where(position < live_count, order, order[jnp.maximum(live_count - 1, 0)])
    live_in_order = (position < live_count).astype(jnp.int32)
    my_writers = (
        lax.dynamic_slice_in_dim(writer_block, my_index * rows_dev, rows_dev, 0)
        - my_index * local_blocks
    )
    writer_match = (my_writers[:, None] == jnp.arange(local_blocks)[None, :])[:, :, None]
    spread = jnp.sum(jnp.where(writer_match, row_grads[:, None, :], 0.0), axis=0) * block_scale
    all_rows = lax.all_to_all(
        jnp.broadcast_to(row_grads[None], (batch_devices, rows_dev, row_width)),
        "batch",
        split_axis=0,
        concat_axis=0,
        tiled=True,
    )
    memory_grad = jnp.sum(all_rows, axis=0)
    memory_grad, qd_all = lax.optimization_barrier((memory_grad, qd_all))
    dk_sum, dv_sum = owner_core(
        src_blk[pick], pick, src_slot[pick], live_in_order, my_slot[pick], qd_all, stats_all,
        key_states[0], value_states[0], spread,
    )
    attended = attended_rows.reshape(1, tokens, row_width)
    query_grad = query_rows_grad.reshape(1, tokens, row_width)
    key_grad = dk_sum.reshape(1, tokens, row_width)
    value_grad = dv_sum.reshape(1, tokens, row_width)
    return (attended, query_grad, key_grad, value_grad, memory_grad)


def solution(mesh):
    placed = (
        P("batch", "seq", None),
        P("batch", "seq", None),
        P("batch", "seq", None),
        P("batch", "seq", None),
        P(),
        P(),
        P(),
        P(),
        P(),
    )
    return jax.shard_map(
        shards,
        mesh=mesh,
        in_specs=placed,
        out_specs=(
            P("batch", "seq", None),
            P("batch", "seq", None),
            P("batch", "seq", None),
            P("batch", "seq", None),
            P("seq", None),
        ),
        check_vma=False,
    )
```

```python
import math

import jax
import jax.numpy as jnp
from jax import lax
from jax.experimental import pallas as pl
from jax.experimental.pallas import tpu as pltpu
from jax.sharding import PartitionSpec as P

HEADS = 8
HD = 128
BLK = 128
MEM = 1024
NEAR = 8


def _rows_of(col):
    eye = lax.broadcasted_iota(jnp.int32, (BLK, BLK), 0) == lax.broadcasted_iota(jnp.int32, (BLK, BLK), 1)
    return jnp.sum(jnp.where(eye, col, 0.0), axis=0, keepdims=True)


def _query_body(cnt_ref, nb_ref, q_ref, do_ref, mk_ref, *rest):
    k_refs = rest[:NEAR]
    v_refs = rest[NEAR : 2 * NEAR]
    o_ref, dq_ref, tm_ref, st_ref = rest[2 * NEAR :]
    n = pl.program_id(0)
    h = pl.program_id(1)
    heads = pl.num_programs(1)
    scale = 1.0 / math.sqrt(HD)
    f32 = jnp.float32
    nt = (((1,), (1,)), ((), ()))
    tn = (((0,), (0,)), ((), ()))
    q = q_ref[...]
    do = do_ref[...]
    mk = mk_ref[...]
    nk = jnp.concatenate([r[...] for r in k_refs], axis=0)
    nv = jnp.concatenate([r[...] for r in v_refs], axis=0)
    sm = lax.dot_general(q, mk, nt, preferred_element_type=f32) * scale
    sn = lax.dot_general(q, nk, nt, preferred_element_type=f32) * scale
    col = lax.broadcasted_iota(jnp.int32, sn.shape, 1) // BLK
    sn = jnp.where(col < cnt_ref[n], sn, -jnp.inf)
    m = jnp.maximum(jnp.max(sm, axis=1, keepdims=True), jnp.max(sn, axis=1, keepdims=True))
    em = jnp.exp(sm - m)
    en = jnp.exp(sn - m)
    total = jnp.sum(em, axis=1, keepdims=True) + jnp.sum(en, axis=1, keepdims=True)
    pm = em / total
    pn = en / total
    wm = pm.astype(jnp.bfloat16)
    wn = pn.astype(jnp.bfloat16)
    o = (
        jnp.dot(wm, mk, preferred_element_type=f32) + jnp.dot(wn, nv, preferred_element_type=f32)
    ).astype(jnp.bfloat16)
    o_ref[...] = o
    gd = jnp.sum(do.astype(f32) * o.astype(f32), axis=1, keepdims=True)
    dpm = lax.dot_general(do, mk, nt, preferred_element_type=f32)
    dpn = lax.dot_general(do, nv, nt, preferred_element_type=f32)
    dsm = (pm * (dpm - gd)).astype(jnp.bfloat16)
    dsn = (pn * (dpn - gd)).astype(jnp.bfloat16)
    dq_ref[...] = (
        (jnp.dot(dsm, mk, preferred_element_type=f32) + jnp.dot(dsn, nk, preferred_element_type=f32))
        * scale
    ).astype(jnp.bfloat16)
    tm_ref[0] = lax.dot_general(dsm, q, tn, preferred_element_type=f32) * scale + lax.dot_general(
        wm, do, tn, preferred_element_type=f32
    )
    st_ref[pl.ds(h, 1), :] = _rows_of(m)
    st_ref[pl.ds(heads + h, 1), :] = _rows_of(total)
    st_ref[pl.ds(2 * heads + h, 1), :] = _rows_of(gd)


def query_core(counts, near_rows, q, do, mk, kv_all):
    tokens, width = q.shape
    blocks = tokens // BLK
    mem = mk.shape[0]
    heads = width // HD
    nrows = NEAR * BLK
    qspec = pl.BlockSpec((BLK, HD), lambda n, h, c, t: (n, h))
    mspec = pl.BlockSpec((mem, HD), lambda n, h, c, t: (0, h))

    def kv_spec(j, which):
        return pl.BlockSpec((BLK, HD), lambda n, h, c, t: (t[n * NEAR + j], which * heads + h))

    flops = 2 * tokens * width * (mem + nrows) * 4 + 2 * tokens * width * (nrows + mem * 2)
    grid_spec = pltpu.PrefetchScalarGridSpec(
        num_scalar_prefetch=2,
        grid=(blocks, heads),
        in_specs=[qspec, qspec, mspec]
        + [kv_spec(j, 0) for j in range(NEAR)]
        + [kv_spec(j, 1) for j in range(NEAR)],
        out_specs=[
            qspec,
            qspec,
            pl.BlockSpec((1, mem, HD), lambda n, h, c, t: (n, 0, h)),
            pl.BlockSpec((3 * heads, BLK), lambda n, h, c, t: (0, n)),
        ],
    )
    return pl.pallas_call(
        _query_body,
        grid_spec=grid_spec,
        out_shape=[
            jax.ShapeDtypeStruct((tokens, width), jnp.bfloat16),
            jax.ShapeDtypeStruct((tokens, width), jnp.bfloat16),
            jax.ShapeDtypeStruct((blocks, mem, width), jnp.float32),
            jax.ShapeDtypeStruct((3 * heads, tokens), jnp.float32),
        ],
        compiler_params=pltpu.CompilerParams(dimension_semantics=("arbitrary", "arbitrary")),
        cost_estimate=pl.CostEstimate(
            flops=flops,
            transcendentals=tokens * heads * (mem + nrows),
            bytes_accessed=2 * (4 * tokens * width + blocks * mem * width + 2 * blocks * nrows * width)
            + 4 * blocks * mem * width,
        ),
    )(counts, near_rows, q, do, mk, *([kv_all] * (2 * NEAR)))


def _owner_body(src_blk, src_dev, src_slot, src_live, my_slot, qd_ref, st_ref, k_ref, v_ref, dk_ref, dv_ref):
    s = pl.program_id(0)
    heads = k_ref.shape[1] // HD
    scale = 1.0 / math.sqrt(HD)
    f32 = jnp.float32
    nt = (((1,), (1,)), ((), ()))

    @pl.when(s == 0)
    def _():
        dk_ref[...] = jnp.zeros(dk_ref.shape, f32)
        dv_ref[...] = jnp.zeros(dv_ref.shape, f32)

    @pl.when(src_live[s] != 0)
    def _():
        rows = pl.ds(pl.multiple_of(my_slot[s] * BLK, BLK), BLK)
        st = st_ref[0]
        for h in range(heads):
            cols = pl.ds(h * HD, HD)
            q_h = qd_ref[:, cols]
            do_h = qd_ref[:, pl.ds((heads + h) * HD, HD)]
            k_h = k_ref[rows, cols]
            v_h = v_ref[rows, cols]
            row_max = st[h : h + 1]
            row_total = st[heads + h : heads + h + 1]
            grad_dot = st[2 * heads + h : 2 * heads + h + 1]
            score_t = lax.dot_general(k_h, q_h, nt, preferred_element_type=f32) * scale
            prob_t = jnp.exp(score_t - row_max) * (1.0 / row_total)
            weight_t = prob_t.astype(jnp.bfloat16)
            dprob_t = lax.dot_general(v_h, do_h, nt, preferred_element_type=f32)
            dscore_t = (prob_t * (dprob_t - grad_dot)).astype(jnp.bfloat16)
            dk = (jnp.dot(dscore_t, q_h, preferred_element_type=f32) * scale).astype(jnp.bfloat16)
            dv = jnp.dot(weight_t, do_h, preferred_element_type=f32).astype(jnp.bfloat16)
            dk_ref[rows, cols] += dk.astype(f32)
            dv_ref[rows, cols] += dv.astype(f32)


def owner_core(src_blk, src_dev, src_slot, src_live, my_slot, qd_all, stats_all, k_loc, v_loc):
    sources = src_blk.shape[0]
    tokens, width = k_loc.shape
    full = pl.BlockSpec((tokens, width), lambda s, a, e, b, c, d: (0, 0))
    grid_spec = pltpu.PrefetchScalarGridSpec(
        num_scalar_prefetch=5,
        grid=(sources,),
        in_specs=[
            pl.BlockSpec((BLK, 2 * width), lambda s, a, e, b, c, d: (a[s], 0)),
            pl.BlockSpec((1, stats_all.shape[1], BLK), lambda s, a, e, b, c, d: (e[s], 0, b[s])),
            full,
            full,
        ],
        out_specs=[full, full],
    )
    return pl.pallas_call(
        _owner_body,
        grid_spec=grid_spec,
        out_shape=[
            jax.ShapeDtypeStruct((tokens, width), jnp.float32),
            jax.ShapeDtypeStruct((tokens, width), jnp.float32),
        ],
        compiler_params=pltpu.CompilerParams(dimension_semantics=("arbitrary",)),
        cost_estimate=pl.CostEstimate(
            flops=sources * 8 * BLK * BLK * width,
            transcendentals=sources * BLK * BLK * (width // HD),
            bytes_accessed=sources * BLK * 2 * width * 2 + 2 * tokens * width * (2 + 8),
        ),
    )(src_blk, src_dev, src_slot, src_live, my_slot, qd_all, stats_all, k_loc, v_loc)


def shards(
    queries,
    key_states,
    value_states,
    out_grad,
    memory,
    near_device,
    near_slot,
    near_count,
    writer_block,
):
    seq_devices = lax.axis_size("seq")
    batch_devices = lax.axis_size("batch")
    my_index = lax.axis_index("seq")
    tokens = queries.shape[1]
    row_width = queries.shape[2]
    local_blocks = tokens // BLK
    rows_dev = MEM // seq_devices
    block_scale = 1.0 / math.sqrt(BLK)
    value_blocks = value_states[0].reshape(local_blocks, BLK, row_width)

    kv_all = lax.all_gather(
        jnp.concatenate([key_states[0], value_states[0]], axis=-1), "seq", axis=0, tiled=True
    )

    value_sums = jnp.sum(value_blocks, axis=1, dtype=jnp.float32)
    all_sums = lax.all_to_all(
        jnp.broadcast_to(value_sums[None], (seq_devices, local_blocks, row_width)),
        "seq",
        split_axis=0,
        concat_axis=0,
        tiled=True,
    ).reshape(seq_devices * local_blocks, row_width)
    memory_keys = (memory + jnp.take(all_sums, writer_block, axis=0) * block_scale).astype(
        jnp.bfloat16
    )
    near_block = (near_device * local_blocks + near_slot).astype(jnp.int32)
    my_near = lax.dynamic_slice_in_dim(near_block, my_index * local_blocks, local_blocks, 0).reshape(-1)
    my_count = lax.dynamic_slice_in_dim(near_count, my_index * local_blocks, local_blocks, 0)
    qd_all = lax.all_gather(
        jnp.concatenate([queries[0], out_grad[0]], axis=-1), "seq", axis=0, tiled=True
    )
    near_width = near_device.shape[1]
    entries = local_blocks * near_width
    target = near_device.reshape(seq_devices, entries)
    source_slot = near_slot.reshape(seq_devices, entries)
    live = (
        jnp.arange(near_width)[None, None, :]
        < near_count.reshape(seq_devices, local_blocks)[:, :, None]
    ).reshape(seq_devices, entries)
    names_me = target == my_index
    entry_at = jnp.argmax(names_me, axis=1).astype(jnp.int32)
    src_slot = entry_at // near_width
    src_blk = (jnp.arange(seq_devices, dtype=jnp.int32) * local_blocks + src_slot).astype(jnp.int32)
    src_live = jnp.any(names_me & live, axis=1).astype(jnp.int32)
    my_slot = jnp.sum(jnp.where(names_me, source_slot, 0), axis=1).astype(jnp.int32)
    order = jnp.argsort(1 - src_live, stable=True).astype(jnp.int32)
    live_count = jnp.sum(src_live)
    position = jnp.arange(seq_devices, dtype=jnp.int32)
    pick = jnp.where(position < live_count, order, order[jnp.maximum(live_count - 1, 0)])
    live_in_order = (position < live_count).astype(jnp.int32)
    t_blk, t_slot, t_my = src_blk[pick], src_slot[pick], my_slot[pick]
    pick, t_blk, t_slot, t_my, live_in_order, memory_keys = lax.optimization_barrier(
        (pick, t_blk, t_slot, t_my, live_in_order, memory_keys)
    )
    attended_rows, query_rows_grad, term, stats = query_core(
        my_count, my_near, queries[0], out_grad[0], memory_keys, kv_all
    )
    stats_all = lax.all_to_all(
        jnp.broadcast_to(stats[None], (seq_devices,) + stats.shape),
        "seq",
        split_axis=0,
        concat_axis=0,
        tiled=True,
    )
    term_rows, qd_all = lax.optimization_barrier((jnp.sum(term, axis=0).astype(jnp.bfloat16), qd_all))
    row_parts = lax.all_to_all(
        term_rows.reshape(seq_devices, rows_dev, row_width),
        "seq",
        split_axis=0,
        concat_axis=0,
        tiled=True,
    )
    row_grads = jnp.sum(row_parts.astype(jnp.float32), axis=0)
    my_writers = (
        lax.dynamic_slice_in_dim(writer_block, my_index * rows_dev, rows_dev, 0)
        - my_index * local_blocks
    )
    writer_match = (my_writers[:, None] == jnp.arange(local_blocks)[None, :])[:, :, None]
    spread = jnp.sum(jnp.where(writer_match, row_grads[:, None, :], 0.0), axis=0) * block_scale
    all_rows = lax.all_to_all(
        jnp.broadcast_to(row_grads[None], (batch_devices, rows_dev, row_width)),
        "batch",
        split_axis=0,
        concat_axis=0,
        tiled=True,
    )
    memory_grad = jnp.sum(all_rows, axis=0)
    dk_sum, dv_sum = owner_core(
        t_blk, pick, t_slot, live_in_order, t_my, qd_all, stats_all,
        key_states[0], value_states[0],
    )
    value_sum = dv_sum.reshape(local_blocks, BLK, row_width)
    attended = attended_rows.reshape(1, tokens, row_width)
    query_grad = query_rows_grad.reshape(1, tokens, row_width)
    key_grad = dk_sum.astype(jnp.bfloat16).reshape(1, tokens, row_width)
    value_grad = (value_sum + spread[:, None, :]).astype(jnp.bfloat16).reshape(1, tokens, row_width)
    return (attended, query_grad, key_grad, value_grad, memory_grad)


def solution(mesh):
    placed = (
        P("batch", "seq", None),
        P("batch", "seq", None),
        P("batch", "seq", None),
        P("batch", "seq", None),
        P(),
        P(),
        P(),
        P(),
        P(),
    )
    return jax.shard_map(
        shards,
        mesh=mesh,
        in_specs=placed,
        out_specs=(
            P("batch", "seq", None),
            P("batch", "seq", None),
            P("batch", "seq", None),
            P("batch", "seq", None),
            P("seq", None),
        ),
        check_vma=False,
    )
```

```python
import math

import jax
import jax.numpy as jnp
from jax import lax
from jax.experimental import pallas as pl
from jax.experimental.pallas import tpu as pltpu
from jax.sharding import PartitionSpec as P

HEADS = 8
HD = 128
BLK = 128
MEM = 1024
NEAR = 8


def _rows_of(col):
    eye = lax.broadcasted_iota(jnp.int32, (BLK, BLK), 0) == lax.broadcasted_iota(jnp.int32, (BLK, BLK), 1)
    return jnp.sum(jnp.where(eye, col, 0.0), axis=0, keepdims=True)


def _query_body(cnt_ref, nb_ref, q_ref, do_ref, mk_ref, *rest):
    k_refs = rest[:NEAR]
    v_refs = rest[NEAR : 2 * NEAR]
    o_ref, dq_ref, tm_ref, st_ref = rest[2 * NEAR :]
    n = pl.program_id(0)
    h = pl.program_id(1)
    heads = pl.num_programs(1)
    scale = 1.0 / math.sqrt(HD)
    f32 = jnp.float32
    nt = (((1,), (1,)), ((), ()))
    tn = (((0,), (0,)), ((), ()))
    q = q_ref[...]
    do = do_ref[...]
    mk = mk_ref[...]
    nk = jnp.concatenate([r[...] for r in k_refs], axis=0)
    nv = jnp.concatenate([r[...] for r in v_refs], axis=0)
    sm = lax.dot_general(q, mk, nt, preferred_element_type=f32) * scale
    sn = lax.dot_general(q, nk, nt, preferred_element_type=f32) * scale
    col = lax.broadcasted_iota(jnp.int32, sn.shape, 1) // BLK
    sn = jnp.where(col < cnt_ref[n], sn, -jnp.inf)
    m = jnp.maximum(jnp.max(sm, axis=1, keepdims=True), jnp.max(sn, axis=1, keepdims=True))
    em = jnp.exp(sm - m)
    en = jnp.exp(sn - m)
    total = jnp.sum(em, axis=1, keepdims=True) + jnp.sum(en, axis=1, keepdims=True)
    pm = em / total
    pn = en / total
    wm = pm.astype(jnp.bfloat16)
    wn = pn.astype(jnp.bfloat16)
    o = (
        jnp.dot(wm, mk, preferred_element_type=f32) + jnp.dot(wn, nv, preferred_element_type=f32)
    ).astype(jnp.bfloat16)
    o_ref[...] = o
    gd = jnp.sum(do.astype(f32) * o.astype(f32), axis=1, keepdims=True)
    dpm = lax.dot_general(do, mk, nt, preferred_element_type=f32)
    dpn = lax.dot_general(do, nv, nt, preferred_element_type=f32)
    dsm = (pm * (dpm - gd)).astype(jnp.bfloat16)
    dsn = (pn * (dpn - gd)).astype(jnp.bfloat16)
    dq_ref[...] = (
        (jnp.dot(dsm, mk, preferred_element_type=f32) + jnp.dot(dsn, nk, preferred_element_type=f32))
        * scale
    ).astype(jnp.bfloat16)
    tm_ref[0] = lax.dot_general(dsm, q, tn, preferred_element_type=f32) * scale + lax.dot_general(
        wm, do, tn, preferred_element_type=f32
    )
    st_ref[pl.ds(h, 1), :] = _rows_of(m)
    st_ref[pl.ds(heads + h, 1), :] = _rows_of(total)
    st_ref[pl.ds(2 * heads + h, 1), :] = _rows_of(gd)


def query_core(counts, near_rows, q, do, mk, kv_all):
    tokens, width = q.shape
    blocks = tokens // BLK
    mem = mk.shape[0]
    heads = width // HD
    nrows = NEAR * BLK
    qspec = pl.BlockSpec((BLK, HD), lambda n, h, c, t: (n, h))
    mspec = pl.BlockSpec((mem, HD), lambda n, h, c, t: (0, h))

    def kv_spec(j, which):
        return pl.BlockSpec((BLK, HD), lambda n, h, c, t: (t[n * NEAR + j], which * heads + h))

    flops = 2 * tokens * width * (mem + nrows) * 4 + 2 * tokens * width * (nrows + mem * 2)
    grid_spec = pltpu.PrefetchScalarGridSpec(
        num_scalar_prefetch=2,
        grid=(blocks, heads),
        in_specs=[qspec, qspec, mspec]
        + [kv_spec(j, 0) for j in range(NEAR)]
        + [kv_spec(j, 1) for j in range(NEAR)],
        out_specs=[
            qspec,
            qspec,
            pl.BlockSpec((1, mem, HD), lambda n, h, c, t: (n, 0, h)),
            pl.BlockSpec((3 * heads, BLK), lambda n, h, c, t: (0, n)),
        ],
    )
    return pl.pallas_call(
        _query_body,
        grid_spec=grid_spec,
        out_shape=[
            jax.ShapeDtypeStruct((tokens, width), jnp.bfloat16),
            jax.ShapeDtypeStruct((tokens, width), jnp.bfloat16),
            jax.ShapeDtypeStruct((blocks, mem, width), jnp.float32),
            jax.ShapeDtypeStruct((3 * heads, tokens), jnp.float32),
        ],
        compiler_params=pltpu.CompilerParams(dimension_semantics=("arbitrary", "arbitrary")),
        cost_estimate=pl.CostEstimate(
            flops=flops,
            transcendentals=tokens * heads * (mem + nrows),
            bytes_accessed=2 * (4 * tokens * width + blocks * mem * width + 2 * blocks * nrows * width)
            + 4 * blocks * mem * width,
        ),
    )(counts, near_rows, q, do, mk, *([kv_all] * (2 * NEAR)))


def _owner_body(src_blk, src_dev, src_slot, src_live, my_slot, qd_ref, st_ref, k_ref, v_ref, dk_ref, dv_ref):
    s = pl.program_id(0)
    heads = k_ref.shape[1] // HD
    scale = 1.0 / math.sqrt(HD)
    f32 = jnp.float32
    nt = (((1,), (1,)), ((), ()))

    @pl.when(s == 0)
    def _():
        dk_ref[...] = jnp.zeros(dk_ref.shape, f32)
        dv_ref[...] = jnp.zeros(dv_ref.shape, f32)

    @pl.when(src_live[s] != 0)
    def _():
        rows = pl.ds(pl.multiple_of(my_slot[s] * BLK, BLK), BLK)
        st = st_ref[0]
        for h in range(heads):
            cols = pl.ds(h * HD, HD)
            q_h = qd_ref[:, cols]
            do_h = qd_ref[:, pl.ds((heads + h) * HD, HD)]
            k_h = k_ref[rows, cols]
            v_h = v_ref[rows, cols]
            row_max = st[h : h + 1]
            row_total = st[heads + h : heads + h + 1]
            grad_dot = st[2 * heads + h : 2 * heads + h + 1]
            score_t = lax.dot_general(k_h, q_h, nt, preferred_element_type=f32) * scale
            prob_t = jnp.exp(score_t - row_max) * (1.0 / row_total)
            weight_t = prob_t.astype(jnp.bfloat16)
            dprob_t = lax.dot_general(v_h, do_h, nt, preferred_element_type=f32)
            dscore_t = (prob_t * (dprob_t - grad_dot)).astype(jnp.bfloat16)
            dk = (jnp.dot(dscore_t, q_h, preferred_element_type=f32) * scale).astype(jnp.bfloat16)
            dv = jnp.dot(weight_t, do_h, preferred_element_type=f32).astype(jnp.bfloat16)
            dk_ref[rows, cols] += dk.astype(f32)
            dv_ref[rows, cols] += dv.astype(f32)


def owner_core(src_blk, src_dev, src_slot, src_live, my_slot, qd_all, stats_all, k_loc, v_loc):
    sources = src_blk.shape[0]
    tokens, width = k_loc.shape
    full = pl.BlockSpec((tokens, width), lambda s, a, e, b, c, d: (0, 0))
    grid_spec = pltpu.PrefetchScalarGridSpec(
        num_scalar_prefetch=5,
        grid=(sources,),
        in_specs=[
            pl.BlockSpec((BLK, 2 * width), lambda s, a, e, b, c, d: (a[s], 0)),
            pl.BlockSpec((1, stats_all.shape[1], BLK), lambda s, a, e, b, c, d: (e[s], 0, 0)),
            full,
            full,
        ],
        out_specs=[full, full],
    )
    return pl.pallas_call(
        _owner_body,
        grid_spec=grid_spec,
        out_shape=[
            jax.ShapeDtypeStruct((tokens, width), jnp.float32),
            jax.ShapeDtypeStruct((tokens, width), jnp.float32),
        ],
        compiler_params=pltpu.CompilerParams(dimension_semantics=("arbitrary",)),
        cost_estimate=pl.CostEstimate(
            flops=sources * 8 * BLK * BLK * width,
            transcendentals=sources * BLK * BLK * (width // HD),
            bytes_accessed=sources * BLK * 2 * width * 2 + 2 * tokens * width * (2 + 8),
        ),
    )(src_blk, src_dev, src_slot, src_live, my_slot, qd_all, stats_all, k_loc, v_loc)


def shards(
    queries,
    key_states,
    value_states,
    out_grad,
    memory,
    near_device,
    near_slot,
    near_count,
    writer_block,
):
    seq_devices = lax.axis_size("seq")
    batch_devices = lax.axis_size("batch")
    my_index = lax.axis_index("seq")
    tokens = queries.shape[1]
    row_width = queries.shape[2]
    local_blocks = tokens // BLK
    rows_dev = MEM // seq_devices
    block_scale = 1.0 / math.sqrt(BLK)
    value_blocks = value_states[0].reshape(local_blocks, BLK, row_width)

    kv_all = lax.all_gather(
        jnp.concatenate([key_states[0], value_states[0]], axis=-1), "seq", axis=0, tiled=True
    )

    value_sums = jnp.sum(value_blocks, axis=1, dtype=jnp.float32)
    all_sums = lax.all_to_all(
        jnp.broadcast_to(value_sums[None], (seq_devices, local_blocks, row_width)),
        "seq",
        split_axis=0,
        concat_axis=0,
        tiled=True,
    ).reshape(seq_devices * local_blocks, row_width)
    memory_keys = (memory + jnp.take(all_sums, writer_block, axis=0) * block_scale).astype(
        jnp.bfloat16
    )
    near_block = (near_device * local_blocks + near_slot).astype(jnp.int32)
    my_near = lax.dynamic_slice_in_dim(near_block, my_index * local_blocks, local_blocks, 0).reshape(-1)
    my_count = lax.dynamic_slice_in_dim(near_count, my_index * local_blocks, local_blocks, 0)
    qd_all = lax.all_gather(
        jnp.concatenate([queries[0], out_grad[0]], axis=-1), "seq", axis=0, tiled=True
    )
    near_width = near_device.shape[1]
    entries = local_blocks * near_width
    target = near_device.reshape(seq_devices, entries)
    source_slot = near_slot.reshape(seq_devices, entries)
    live = (
        jnp.arange(near_width)[None, None, :]
        < near_count.reshape(seq_devices, local_blocks)[:, :, None]
    ).reshape(seq_devices, entries)
    names_me = target == my_index
    entry_at = jnp.argmax(names_me, axis=1).astype(jnp.int32)
    src_slot = entry_at // near_width
    src_blk = (jnp.arange(seq_devices, dtype=jnp.int32) * local_blocks + src_slot).astype(jnp.int32)
    src_live = jnp.any(names_me & live, axis=1).astype(jnp.int32)
    my_slot = jnp.sum(jnp.where(names_me, source_slot, 0), axis=1).astype(jnp.int32)
    order = jnp.argsort(1 - src_live, stable=True).astype(jnp.int32)
    live_count = jnp.sum(src_live)
    position = jnp.arange(seq_devices, dtype=jnp.int32)
    pick = jnp.where(position < live_count, order, order[jnp.maximum(live_count - 1, 0)])
    live_in_order = (position < live_count).astype(jnp.int32)
    t_blk, t_slot, t_my = src_blk[pick], src_slot[pick], my_slot[pick]
    pick, t_blk, t_slot, t_my, live_in_order, memory_keys = lax.optimization_barrier(
        (pick, t_blk, t_slot, t_my, live_in_order, memory_keys)
    )
    attended_rows, query_rows_grad, term, stats = query_core(
        my_count, my_near, queries[0], out_grad[0], memory_keys, kv_all
    )
    mine = lax.dynamic_slice_in_dim(near_device, my_index * local_blocks, local_blocks, 0).reshape(-1)
    hit = mine[None, :] == jnp.arange(seq_devices)[:, None]
    send_block = jnp.sum(jnp.where(hit, jnp.arange(mine.shape[0])[None, :] // near_device.shape[1], 0), axis=1)
    stats_send = jnp.take(stats.reshape(stats.shape[0], local_blocks, BLK), send_block, axis=1)
    stats_all = lax.all_to_all(
        jnp.transpose(stats_send, (1, 0, 2)),
        "seq",
        split_axis=0,
        concat_axis=0,
        tiled=True,
    )
    term_rows, qd_all = lax.optimization_barrier((jnp.sum(term, axis=0).astype(jnp.bfloat16), qd_all))
    row_parts = lax.all_to_all(
        term_rows.reshape(seq_devices, rows_dev, row_width),
        "seq",
        split_axis=0,
        concat_axis=0,
        tiled=True,
    )
    row_grads = jnp.sum(row_parts.astype(jnp.float32), axis=0)
    my_writers = (
        lax.dynamic_slice_in_dim(writer_block, my_index * rows_dev, rows_dev, 0)
        - my_index * local_blocks
    )
    writer_match = (my_writers[:, None] == jnp.arange(local_blocks)[None, :])[:, :, None]
    spread = jnp.sum(jnp.where(writer_match, row_grads[:, None, :], 0.0), axis=0) * block_scale
    all_rows = lax.all_to_all(
        jnp.broadcast_to(row_grads[None], (batch_devices, rows_dev, row_width)),
        "batch",
        split_axis=0,
        concat_axis=0,
        tiled=True,
    )
    memory_grad = jnp.sum(all_rows, axis=0)
    dk_sum, dv_sum = owner_core(
        t_blk, pick, t_slot, live_in_order, t_my, qd_all, stats_all,
        key_states[0], value_states[0],
    )
    value_sum = dv_sum.reshape(local_blocks, BLK, row_width)
    attended = attended_rows.reshape(1, tokens, row_width)
    query_grad = query_rows_grad.reshape(1, tokens, row_width)
    key_grad = dk_sum.astype(jnp.bfloat16).reshape(1, tokens, row_width)
    value_grad = (value_sum + spread[:, None, :]).astype(jnp.bfloat16).reshape(1, tokens, row_width)
    return (attended, query_grad, key_grad, value_grad, memory_grad)


def solution(mesh):
    placed = (
        P("batch", "seq", None),
        P("batch", "seq", None),
        P("batch", "seq", None),
        P("batch", "seq", None),
        P(),
        P(),
        P(),
        P(),
        P(),
    )
    return jax.shard_map(
        shards,
        mesh=mesh,
        in_specs=placed,
        out_specs=(
            P("batch", "seq", None),
            P("batch", "seq", None),
            P("batch", "seq", None),
            P("batch", "seq", None),
            P("seq", None),
        ),
        check_vma=False,
    )
```

```python
import math

import jax
import jax.numpy as jnp
from jax import lax
from jax.experimental import pallas as pl
from jax.experimental.pallas import tpu as pltpu
from jax.sharding import PartitionSpec as P

HEADS = 8
HD = 128
BLK = 128
MEM = 1024
NEAR = 8


def _rows_of(col):
    eye = lax.broadcasted_iota(jnp.int32, (BLK, BLK), 0) == lax.broadcasted_iota(jnp.int32, (BLK, BLK), 1)
    return jnp.sum(jnp.where(eye, col, 0.0), axis=0, keepdims=True)


def _query_body(cnt_ref, nb_ref, q_ref, do_ref, mk_ref, *rest):
    k_refs = rest[:NEAR]
    v_refs = rest[NEAR : 2 * NEAR]
    o_ref, dq_ref, tm_ref, st_ref = rest[2 * NEAR :]
    n = pl.program_id(0)
    h = pl.program_id(1)
    heads = pl.num_programs(1)
    scale = 1.0 / math.sqrt(HD)
    f32 = jnp.float32
    nt = (((1,), (1,)), ((), ()))
    tn = (((0,), (0,)), ((), ()))
    q = q_ref[...]
    do = do_ref[...]
    mk = mk_ref[...]
    nk = jnp.concatenate([r[...] for r in k_refs], axis=0)
    nv = jnp.concatenate([r[...] for r in v_refs], axis=0)
    sm = lax.dot_general(q, mk, nt, preferred_element_type=f32) * scale
    sn = lax.dot_general(q, nk, nt, preferred_element_type=f32) * scale
    col = lax.broadcasted_iota(jnp.int32, sn.shape, 1) // BLK
    sn = jnp.where(col < cnt_ref[n], sn, -jnp.inf)
    m = jnp.maximum(jnp.max(sm, axis=1, keepdims=True), jnp.max(sn, axis=1, keepdims=True))
    em = jnp.exp(sm - m)
    en = jnp.exp(sn - m)
    total = jnp.sum(em, axis=1, keepdims=True) + jnp.sum(en, axis=1, keepdims=True)
    pm = em / total
    pn = en / total
    wm = pm.astype(jnp.bfloat16)
    wn = pn.astype(jnp.bfloat16)
    o = (
        jnp.dot(wm, mk, preferred_element_type=f32) + jnp.dot(wn, nv, preferred_element_type=f32)
    ).astype(jnp.bfloat16)
    o_ref[...] = o
    gd = jnp.sum(do.astype(f32) * o.astype(f32), axis=1, keepdims=True)
    dpm = lax.dot_general(do, mk, nt, preferred_element_type=f32)
    dpn = lax.dot_general(do, nv, nt, preferred_element_type=f32)
    dsm = (pm * (dpm - gd)).astype(jnp.bfloat16)
    dsn = (pn * (dpn - gd)).astype(jnp.bfloat16)
    dq_ref[...] = (
        (jnp.dot(dsm, mk, preferred_element_type=f32) + jnp.dot(dsn, nk, preferred_element_type=f32))
        * scale
    ).astype(jnp.bfloat16)
    tm_ref[0] = lax.dot_general(dsm, q, tn, preferred_element_type=f32) * scale + lax.dot_general(
        wm, do, tn, preferred_element_type=f32
    )
    st_ref[pl.ds(h, 1), :] = _rows_of(m)
    st_ref[pl.ds(heads + h, 1), :] = _rows_of(total)
    st_ref[pl.ds(2 * heads + h, 1), :] = _rows_of(gd)


def query_core(counts, near_rows, q, do, mk, kv_all):
    tokens, width = q.shape
    blocks = tokens // BLK
    mem = mk.shape[0]
    heads = width // HD
    nrows = NEAR * BLK
    qspec = pl.BlockSpec((BLK, HD), lambda n, h, c, t: (n, h))
    mspec = pl.BlockSpec((mem, HD), lambda n, h, c, t: (0, h))

    def kv_spec(j, which):
        return pl.BlockSpec((BLK, HD), lambda n, h, c, t: (t[n * NEAR + j], which * heads + h))

    flops = 2 * tokens * width * (mem + nrows) * 4 + 2 * tokens * width * (nrows + mem * 2)
    grid_spec = pltpu.PrefetchScalarGridSpec(
        num_scalar_prefetch=2,
        grid=(blocks, heads),
        in_specs=[qspec, qspec, mspec]
        + [kv_spec(j, 0) for j in range(NEAR)]
        + [kv_spec(j, 1) for j in range(NEAR)],
        out_specs=[
            qspec,
            qspec,
            pl.BlockSpec((1, mem, HD), lambda n, h, c, t: (n, 0, h)),
            pl.BlockSpec((3 * heads, BLK), lambda n, h, c, t: (0, n)),
        ],
    )
    return pl.pallas_call(
        _query_body,
        grid_spec=grid_spec,
        out_shape=[
            jax.ShapeDtypeStruct((tokens, width), jnp.bfloat16),
            jax.ShapeDtypeStruct((tokens, width), jnp.bfloat16),
            jax.ShapeDtypeStruct((blocks, mem, width), jnp.float32),
            jax.ShapeDtypeStruct((3 * heads, tokens), jnp.float32),
        ],
        compiler_params=pltpu.CompilerParams(dimension_semantics=("arbitrary", "arbitrary")),
        cost_estimate=pl.CostEstimate(
            flops=flops,
            transcendentals=tokens * heads * (mem + nrows),
            bytes_accessed=2 * (4 * tokens * width + blocks * mem * width + 2 * blocks * nrows * width)
            + 4 * blocks * mem * width,
        ),
    )(counts, near_rows, q, do, mk, *([kv_all] * (2 * NEAR)))


def _owner_body(src_blk, src_dev, src_slot, src_live, my_slot, qd_ref, st_ref, k_ref, v_ref, dk_ref, dv_ref):
    s = pl.program_id(0)
    heads = k_ref.shape[1] // HD
    scale = 1.0 / math.sqrt(HD)
    f32 = jnp.float32
    nt = (((1,), (1,)), ((), ()))

    @pl.when(s == 0)
    def _():
        dk_ref[...] = jnp.zeros(dk_ref.shape, f32)
        dv_ref[...] = jnp.zeros(dv_ref.shape, f32)

    @pl.when(src_live[s] != 0)
    def _():
        rows = pl.ds(pl.multiple_of(my_slot[s] * BLK, BLK), BLK)
        st = st_ref[0]
        for h in range(heads):
            cols = pl.ds(h * HD, HD)
            q_h = qd_ref[:, cols]
            do_h = qd_ref[:, pl.ds((heads + h) * HD, HD)]
            k_h = k_ref[rows, cols]
            v_h = v_ref[rows, cols]
            row_max = st[h : h + 1]
            row_total = st[heads + h : heads + h + 1]
            grad_dot = st[2 * heads + h : 2 * heads + h + 1]
            score_t = lax.dot_general(k_h, q_h, nt, preferred_element_type=f32) * scale
            prob_t = jnp.exp(score_t - row_max) * (1.0 / row_total)
            weight_t = prob_t.astype(jnp.bfloat16)
            dprob_t = lax.dot_general(v_h, do_h, nt, preferred_element_type=f32)
            dscore_t = (prob_t * (dprob_t - grad_dot)).astype(jnp.bfloat16)
            dk = (jnp.dot(dscore_t, q_h, preferred_element_type=f32) * scale).astype(jnp.bfloat16)
            dv = jnp.dot(weight_t, do_h, preferred_element_type=f32).astype(jnp.bfloat16)
            dk_ref[rows, cols] += dk.astype(f32)
            dv_ref[rows, cols] += dv.astype(f32)


def owner_core(src_blk, src_dev, src_slot, src_live, my_slot, qd_all, stats_all, k_loc, v_loc):
    sources = src_blk.shape[0]
    tokens, width = k_loc.shape
    full = pl.BlockSpec((tokens, width), lambda s, a, e, b, c, d: (0, 0))
    grid_spec = pltpu.PrefetchScalarGridSpec(
        num_scalar_prefetch=5,
        grid=(sources,),
        in_specs=[
            pl.BlockSpec((BLK, 2 * width), lambda s, a, e, b, c, d: (a[s], 0)),
            pl.BlockSpec((1, stats_all.shape[1], BLK), lambda s, a, e, b, c, d: (e[s], 0, b[s])),
            full,
            full,
        ],
        out_specs=[full, full],
    )
    return pl.pallas_call(
        _owner_body,
        grid_spec=grid_spec,
        out_shape=[
            jax.ShapeDtypeStruct((tokens, width), jnp.float32),
            jax.ShapeDtypeStruct((tokens, width), jnp.float32),
        ],
        compiler_params=pltpu.CompilerParams(dimension_semantics=("arbitrary",)),
        cost_estimate=pl.CostEstimate(
            flops=sources * 8 * BLK * BLK * width,
            transcendentals=sources * BLK * BLK * (width // HD),
            bytes_accessed=sources * BLK * 2 * width * 2 + 2 * tokens * width * (2 + 8),
        ),
    )(src_blk, src_dev, src_slot, src_live, my_slot, qd_all, stats_all, k_loc, v_loc)


def shards(
    queries,
    key_states,
    value_states,
    out_grad,
    memory,
    near_device,
    near_slot,
    near_count,
    writer_block,
):
    seq_devices = lax.axis_size("seq")
    batch_devices = lax.axis_size("batch")
    my_index = lax.axis_index("seq")
    tokens = queries.shape[1]
    row_width = queries.shape[2]
    local_blocks = tokens // BLK
    rows_dev = MEM // seq_devices
    block_scale = 1.0 / math.sqrt(BLK)
    value_blocks = value_states[0].reshape(local_blocks, BLK, row_width)

    kv_all = lax.all_gather(
        jnp.concatenate([key_states[0], value_states[0]], axis=-1), "seq", axis=0, tiled=True
    )

    value_sums = jnp.sum(value_blocks, axis=1, dtype=jnp.float32)
    all_sums = lax.all_to_all(
        jnp.broadcast_to(value_sums[None], (seq_devices, local_blocks, row_width)),
        "seq",
        split_axis=0,
        concat_axis=0,
        tiled=True,
    ).reshape(seq_devices * local_blocks, row_width)
    memory_keys = (memory + jnp.take(all_sums, writer_block, axis=0) * block_scale).astype(
        jnp.bfloat16
    )
    near_block = (near_device * local_blocks + near_slot).astype(jnp.int32)
    my_near = lax.dynamic_slice_in_dim(near_block, my_index * local_blocks, local_blocks, 0).reshape(-1)
    my_count = lax.dynamic_slice_in_dim(near_count, my_index * local_blocks, local_blocks, 0)
    qd_all = lax.all_gather(
        jnp.concatenate([queries[0], out_grad[0]], axis=-1), "seq", axis=0, tiled=True
    )
    near_width = near_device.shape[1]
    entries = local_blocks * near_width
    target = near_device.reshape(seq_devices, entries)
    source_slot = near_slot.reshape(seq_devices, entries)
    live = (
        jnp.arange(near_width)[None, None, :]
        < near_count.reshape(seq_devices, local_blocks)[:, :, None]
    ).reshape(seq_devices, entries)
    names_me = target == my_index
    entry_at = jnp.argmax(names_me, axis=1).astype(jnp.int32)
    src_slot = entry_at // near_width
    src_blk = (jnp.arange(seq_devices, dtype=jnp.int32) * local_blocks + src_slot).astype(jnp.int32)
    src_live = jnp.any(names_me & live, axis=1).astype(jnp.int32)
    my_slot = jnp.sum(jnp.where(names_me, source_slot, 0), axis=1).astype(jnp.int32)
    order = jnp.argsort(1 - src_live, stable=True).astype(jnp.int32)
    live_count = jnp.sum(src_live)
    position = jnp.arange(seq_devices, dtype=jnp.int32)
    pick = jnp.where(position < live_count, order, order[jnp.maximum(live_count - 1, 0)])
    live_in_order = (position < live_count).astype(jnp.int32)
    t_blk, t_slot, t_my = src_blk[pick], src_slot[pick], my_slot[pick]
    pick, t_blk, t_slot, t_my, live_in_order, memory_keys = lax.optimization_barrier(
        (pick, t_blk, t_slot, t_my, live_in_order, memory_keys)
    )
    attended_rows, query_rows_grad, term, stats = query_core(
        my_count, my_near, queries[0], out_grad[0], memory_keys, kv_all
    )
    stats_all = lax.all_to_all(
        jnp.broadcast_to(stats[None], (seq_devices,) + stats.shape),
        "seq",
        split_axis=0,
        concat_axis=0,
        tiled=True,
    )
    term_rows, qd_all = lax.optimization_barrier((jnp.sum(term, axis=0).astype(jnp.bfloat16), qd_all))
    row_parts = lax.all_to_all(
        term_rows.reshape(seq_devices, rows_dev, row_width),
        "seq",
        split_axis=0,
        concat_axis=0,
        tiled=True,
    )
    row_grads = jnp.sum(row_parts.astype(jnp.float32), axis=0)
    my_writers = (
        lax.dynamic_slice_in_dim(writer_block, my_index * rows_dev, rows_dev, 0)
        - my_index * local_blocks
    )
    writer_match = (my_writers[:, None] == jnp.arange(local_blocks)[None, :])[:, :, None]
    spread = jnp.sum(jnp.where(writer_match, row_grads[:, None, :], 0.0), axis=0) * block_scale
    all_rows = lax.all_to_all(
        jnp.broadcast_to(row_grads.astype(jnp.bfloat16)[None], (batch_devices, rows_dev, row_width)),
        "batch",
        split_axis=0,
        concat_axis=0,
        tiled=True,
    )
    memory_grad = jnp.sum(all_rows.astype(jnp.float32), axis=0)
    dk_sum, dv_sum = owner_core(
        t_blk, pick, t_slot, live_in_order, t_my, qd_all, stats_all,
        key_states[0], value_states[0],
    )
    value_sum = dv_sum.reshape(local_blocks, BLK, row_width)
    attended = attended_rows.reshape(1, tokens, row_width)
    query_grad = query_rows_grad.reshape(1, tokens, row_width)
    key_grad = dk_sum.astype(jnp.bfloat16).reshape(1, tokens, row_width)
    value_grad = (value_sum + spread[:, None, :]).astype(jnp.bfloat16).reshape(1, tokens, row_width)
    return (attended, query_grad, key_grad, value_grad, memory_grad)


def solution(mesh):
    placed = (
        P("batch", "seq", None),
        P("batch", "seq", None),
        P("batch", "seq", None),
        P("batch", "seq", None),
        P(),
        P(),
        P(),
        P(),
        P(),
    )
    return jax.shard_map(
        shards,
        mesh=mesh,
        in_specs=placed,
        out_specs=(
            P("batch", "seq", None),
            P("batch", "seq", None),
            P("batch", "seq", None),
            P("batch", "seq", None),
            P("seq", None),
        ),
        check_vma=False,
    )
```
